256 devices in a mesh: frame: 32 (over x, z), row: 8 (over y, core).
Axes of the slice: x: 4, y: 4, z: 8, core: 2. Of those that a mesh axis runs over, the one named last changes fastest.
Arguments:
- query_in: bfloat16 [128, 8, 32, 2240], P('frame', 'row'), may hold values from -6 to 6
- key_in: bfloat16 [128, 8, 32, 2240], P('frame', 'row'), may hold values from -24 to 24, as said below
- value_in: bfloat16 [128, 8, 32, 2240], P('frame', 'row'), may hold values from -32 to 32, as said below
- hidden_in: bfloat16 [128, 8, 32, 2240], P('frame', 'row'), may hold values from -16 to 16, as said below
- out_weight: bfloat16 [2240, 2240], replicated, may hold values from -0.125 to 0.125
- norm_gain: float32 [2240], replicated, may hold values from 0.25 to 1.75
- temporal_taps: float32 [3, 2240], replicated, may hold values from -3.5 to 3.5
- block_valid: int32 [32], P('frame'), may hold values from 1 to 4, as said below
Outputs:
- mixed: bfloat16 [128, 8, 32, 2240], P('frame', 'row')
The draws below stay inside these ranges and needn't reach their ends.
Inputs may be any that keep to these rules, and one draw needn't show every extreme that they name: key_in lies within this range. value_in lies within this range. hidden_in lies within this range. `block_valid`: the first frame block is full.
All inputs are finite; a program needn't handle non-finite values.
Results may differ from the reference program's by a relative error of at most 0.0058.
Values may be sent and summed in bfloat16 or wider, within the bound.
No kernel may reach another device: no remote copies, remote signals or barrier semaphores. Data moves between devices by JAX's collectives and lax.ppermute only.
A program may use at most 128 MiB of HBM per device.

```python
import math
import jax
import jax.numpy as jnp
from jax import lax

D = 2240
HEADS = 20
DH = 112
FB = 4
KT = 3
F = 128
HR = 8
WC = 32
N_FRAME = 32


def head_order(order_key):
    return jax.random.permutation(order_key, DH)


def tied_fields(key):
    noise_key, scale_key, order_key = jax.random.split(jax.random.fold_in(key, 11), 3)
    blocks = F // FB
    shape_full = (blocks, FB, HR, WC, HEADS, DH)
    raw_field = jnp.clip(jax.random.normal(noise_key, shape_full, jnp.float32), -4.0, 4.0)
    log_scale = jax.random.uniform(scale_key, (blocks, 1, HR, 1, HEADS, 1), jnp.float32, math.log(0.3), math.log(3.0))
    centre = 0.0293
    strength = 8.0
    key_field = jnp.exp(log_scale) * (raw_field - 1.5)
    feature = jnp.maximum(raw_field - 1.5, 0.0) - centre
    orders = jax.vmap(head_order)(jax.random.split(order_key, HEADS))
    head_index = jnp.arange(HEADS)[:, None]
    tied_part = strength * feature[:, :, :, :, head_index, orders]
    return (key_field.reshape(F, HR, WC, D), tied_part.reshape(F, HR, WC, D))


def draw_key_in(key, part):
    key_field, tied_part = tied_fields(key)
    return key_field.astype(jnp.bfloat16)


def draw_value_in(key, part):
    key_field, tied_part = tied_fields(key)
    noise_key, shared_key = jax.random.split(jax.random.fold_in(key, 23), 2)
    blocks = F // FB
    shape_full = (blocks, FB, HR, WC, D)
    shared = jnp.clip(jax.random.normal(shared_key, (blocks, 1, HR, 1, D), jnp.float32), -4.0, 4.0)
    noise_field = jnp.clip(jax.random.normal(noise_key, shape_full, jnp.float32), -4.0, 4.0)
    values_full = noise_field + 1.5 * shared
    return (values_full.reshape(F, HR, WC, D) + tied_part).astype(jnp.bfloat16)


def draw_hidden_in(key, part):
    noise_key, row_key, column_key = jax.random.split(jax.random.fold_in(key, 37), 3)
    row_scale = jnp.exp(jax.random.uniform(row_key, (F, HR, WC, 1), jnp.float32, math.log(0.2), math.log(2.0)))
    column_scale = jnp.exp(jax.random.uniform(column_key, (1, 1, 1, D), jnp.float32, math.log(0.2), math.log(2.0)))
    noise_field = jnp.clip(jax.random.normal(noise_key, (F, HR, WC, D), jnp.float32), -4.0, 4.0)
    field = noise_field * row_scale * column_scale
    return field.astype(jnp.bfloat16)


def draw_block_valid(key, part):
    counts = jax.random.randint(jax.random.fold_in(key, 51), (N_FRAME,), 1, FB + 1)
    return jnp.where(jnp.arange(N_FRAME) == 0, FB, counts).astype(jnp.int32)


def levels(stream_key, dims, cuts, low, top_value):
    level, own = 1.0, jax.random.fold_in(stream_key, 6)
    for dim, blocks in cuts:
        draws = jnp.exp(jax.random.uniform(jax.random.fold_in(own, dim), (blocks,), jnp.float32, low / len(cuts), top_value / len(cuts)))
        level = level * jnp.repeat(draws, dims[dim] // blocks).reshape([-1 if axis == dim else 1 for axis in range(len(dims))])
    return level


def noise(rng, dims, scale, bound, cuts=(), kind=jnp.bfloat16):
    entries = scale * jax.random.normal(rng, dims, jnp.float32)
    if cuts:
        entries = entries * levels(rng, dims, cuts, -0.22, 0.18)
    return jnp.clip(entries, -bound, bound).astype(kind)


def setup_inputs(seed: int = 0) -> dict:
    keys = jax.random.split(jax.random.key(seed), 9)
    return {
        "query_in": noise(keys[0], (F, HR, WC, D), 1.0, 6.0, ((0, 32), (1, 8))),
        "key_in": draw_key_in(jax.random.fold_in(keys[8], 71), 0),
        "value_in": draw_value_in(jax.random.fold_in(keys[8], 71), 0),
        "hidden_in": draw_hidden_in(jax.random.fold_in(keys[8], 71), 0),
        "out_weight": noise(keys[4], (D, D), D ** -0.5, 0.125),
        "norm_gain": jnp.clip(1.0 + 0.15 * jax.random.normal(keys[5], (D,), jnp.float32), 0.25, 1.75),
        "temporal_taps": noise(keys[6], (KT, D), KT ** -0.5, 3.5, (), jnp.float32),
        "block_valid": draw_block_valid(jax.random.fold_in(keys[8], 71), 0),
    }


EPS_DEN = 1e-06
EPS_NORM = 1e-06

def reference(query_in, key_in, value_in, hidden_in, out_weight, norm_gain, temporal_taps, block_valid):
    highest = lax.Precision.HIGHEST
    frame_pos = jnp.tile(jnp.arange(FB, dtype=jnp.int32), N_FRAME)
    frame_limit = jnp.repeat(block_valid, FB)
    frame_mask = (frame_pos < frame_limit).astype(jnp.float32)
    block_mask = frame_mask.reshape(N_FRAME, FB)
    block_ids = jnp.arange(N_FRAME, dtype=jnp.int32)

    def block_state(block_index):
        anchor = (block_index * FB).astype(jnp.int32)
        key_block = lax.dynamic_slice_in_dim(key_in, anchor, FB, 0).astype(jnp.float32)
        value_block = lax.dynamic_slice_in_dim(value_in, anchor, FB, 0).astype(jnp.float32)
        frame_weight = lax.dynamic_index_in_dim(block_mask, block_index, 0, keepdims=False)
        key_feat = (jnp.maximum(key_block, 0.0) * frame_weight[:, None, None, None]).reshape(-1, HEADS, DH)
        value_feat = value_block.reshape(-1, HEADS, DH)
        local_state = jnp.einsum('thi,thj->hij', key_feat, value_feat, precision=highest)
        local_norm = lax.optimization_barrier(jnp.sum(key_feat, axis=0))
        return (local_state, local_norm)
    states, norms = lax.map(block_state, block_ids)
    total_states = jnp.cumsum(states, axis=0).astype(jnp.bfloat16)
    total_norms = jnp.cumsum(norms, axis=0).astype(jnp.bfloat16)

    def block_output(block_index):
        anchor = (block_index * FB).astype(jnp.int32)
        query_block = lax.dynamic_slice_in_dim(query_in, anchor, FB, 0).astype(jnp.float32)
        hidden_block = lax.dynamic_slice_in_dim(hidden_in, anchor, FB, 0)
        frame_weight = lax.dynamic_index_in_dim(block_mask, block_index, 0, keepdims=False)
        state_now = lax.dynamic_index_in_dim(total_states, block_index, 0, keepdims=False).astype(jnp.float32)
        norm_now = lax.dynamic_index_in_dim(total_norms, block_index, 0, keepdims=False).astype(jnp.float32)
        query_feat = jnp.maximum(query_block, 0.0).reshape(-1, HEADS, DH)
        numerator = jnp.einsum('thi,hij->thj', query_feat, state_now, precision=highest)
        denominator = jnp.einsum('thi,hi->th', query_feat, norm_now, precision=highest) + EPS_DEN
        token_mask = jnp.broadcast_to(frame_weight[:, None, None], (FB, HR, WC)).reshape(-1, 1, 1)
        attended = (numerator / denominator[:, :, None] * token_mask).reshape(-1, D).astype(jnp.bfloat16)
        projected = jnp.dot(attended, out_weight, preferred_element_type=jnp.float32)
        residual = (hidden_block.reshape(-1, D).astype(jnp.float32) + projected).astype(jnp.bfloat16)
        residual_f = lax.optimization_barrier(residual).astype(jnp.float32)
        inverse = lax.rsqrt(lax.optimization_barrier(jnp.mean(residual_f * residual_f, axis=-1, keepdims=True)) + EPS_NORM)
        normed = (residual_f * inverse * norm_gain).astype(jnp.bfloat16)
        return (residual.reshape(FB, HR, WC, D), normed.reshape(FB, HR, WC, D))
    residuals, normeds = lax.map(block_output, block_ids)
    residual_all = residuals.reshape(F, HR, WC, D)
    normed_all = normeds.reshape(F, HR, WC, D)
    leading = jnp.zeros((KT - 1, HR, WC, D), jnp.bfloat16)
    extended = jnp.concatenate([leading, normed_all], axis=0)
    temporal = jnp.zeros((F, HR, WC, D), jnp.float32)
    for offset in range(KT):
        lower = KT - 1 - offset
        temporal = temporal + temporal_taps[offset] * extended[lower:lower + F].astype(jnp.float32)
    temporal = temporal.astype(jnp.bfloat16)
    temporal_f = lax.optimization_barrier(temporal).astype(jnp.float32)
    return (residual_all.astype(jnp.float32) + temporal_f).astype(jnp.bfloat16)
```

```python
import functools

import jax
import jax.numpy as jnp
from jax import lax
from jax.experimental import pallas as pl
from jax.experimental.pallas import tpu as pltpu
from jax.sharding import Mesh, PartitionSpec as P

HEADS = 20
DH = 112
LANES = 128
PIECE = 14
GROUP = HEADS // 2
ROWS = 1024
EPS_DEN = 1e-06
EPS_NORM = 1e-06
X, Z, Y, C = 4, 8, 4, 2


def smem():
    return pl.BlockSpec(memory_space=pltpu.SMEM)


def vmem():
    return pl.BlockSpec(memory_space=pltpu.VMEM)


def lane_of(shape):
    return lax.broadcasted_iota(jnp.int32, shape, 1)


def state_kernel(core_ref, valid_ref, key_ref, value_ref, keep_ref, send_ref, both):
    tokens = key_ref.shape[0]
    row = lax.broadcasted_iota(jnp.int32, (tokens, DH), 0)
    live = row < valid_ref[0] * 32
    lane = lane_of((tokens, LANES))
    pad = jnp.zeros((tokens, LANES - DH), jnp.bfloat16)

    def head(h):
        keys = key_ref[:, h * DH : (h + 1) * DH]
        values = value_ref[:, h * DH : (h + 1) * DH]
        keys = jnp.where(live, jnp.maximum(keys, 0), jnp.zeros_like(keys))
        values = jnp.concatenate([values, pad], axis=1)
        values = jnp.where(lane == DH, jnp.ones_like(values), values)
        return lax.dot_general(
            keys, values, (((0,), (0,)), ((), ())), preferred_element_type=jnp.float32
        )

    lanes = lane_of((DH, LANES))
    for group in range(2):
        place = (core_ref[0] + group) % 2
        last = head(group * GROUP + GROUP - 1)
        for p in range(GROUP - 1):
            state = head(group * GROUP + p)
            if p < 8:
                moved = pltpu.roll(last, (114 - PIECE * p) % LANES, axis=1)
                state = jnp.where(lanes >= 114, moved, state)
            else:
                state = jnp.where(lanes == 113, pltpu.roll(last, 1, axis=1), state)
            both[place, p * DH : (p + 1) * DH, :] = state
        both[place, (GROUP - 1) * DH :, :] = jnp.zeros((ROWS - (GROUP - 1) * DH, LANES), jnp.float32)
    keep_ref[...] = both[0]
    send_ref[...] = both[1].astype(jnp.bfloat16)


def local_states(core, valid, key, value):
    return pl.pallas_call(
        state_kernel,
        out_shape=(
            jax.ShapeDtypeStruct((ROWS, LANES), jnp.float32),
            jax.ShapeDtypeStruct((ROWS, LANES), jnp.bfloat16),
        ),
        in_specs=[smem(), smem(), vmem(), vmem()],
        out_specs=(vmem(), vmem()),
        scratch_shapes=[pltpu.VMEM((2, ROWS, LANES), jnp.float32)],
        name="local_states",
    )(core, valid, key, value)


def prefix_kernel(got_ref, prefix_ref, whole_ref):
    total = jnp.zeros(whole_ref.shape, jnp.float32)
    for z in range(Z):
        for y in range(Y):
            total = total + got_ref[z * Y + y].astype(jnp.float32)
        prefix_ref[z] = total
    whole_ref[...] = total


def prefixes(got):
    piece = got.shape[1:]
    return pl.pallas_call(
        prefix_kernel,
        out_shape=(
            jax.ShapeDtypeStruct((Z,) + piece, jnp.float32),
            jax.ShapeDtypeStruct(piece, jnp.float32),
        ),
        in_specs=[vmem()],
        out_specs=(vmem(), vmem()),
        name="prefixes",
    )(got)


def totals_kernel(prefix_ref, a_ref, b_ref, c_ref, out_ref):
    before = a_ref[...] + b_ref[...] + c_ref[...]
    for z in range(Z):
        total = (prefix_ref[z] + before).astype(jnp.bfloat16)
        for y in range(Y):
            out_ref[z * Y + y] = total


def totals(prefix, a, b, c):
    piece = prefix.shape[1:]
    return pl.pallas_call(
        totals_kernel,
        out_shape=jax.ShapeDtypeStruct((Z * Y,) + piece, jnp.bfloat16),
        in_specs=[vmem()] * 4,
        out_specs=vmem(),
        name="totals",
    )(prefix, a, b, c)


def attend_kernel(core_ref, valid_ref, own_ref, other_ref, query_ref, out_ref, both):
    tokens = query_ref.shape[0]
    own = core_ref[0]
    both[own] = own_ref[...]
    both[1 - own] = other_ref[...]
    row = lax.broadcasted_iota(jnp.int32, (tokens, 1), 0)
    live = (row < valid_ref[0] * 32).astype(jnp.float32)
    lanes = lane_of((DH, LANES))
    for group in range(2):
        packed = [both[group, p * DH : (p + 1) * DH, :].astype(jnp.float32) for p in range(GROUP - 1)]
        last = jnp.where(lanes == DH, pltpu.roll(packed[8], LANES - 1, axis=1), 0.0)
        for p in range(8):
            moved = pltpu.roll(packed[p], (PIECE * p - 114) % LANES, axis=1)
            last = jnp.where((lanes >= PIECE * p) & (lanes < PIECE * (p + 1)), moved, last)
        for p in range(GROUP):
            state = (packed[p] if p < GROUP - 1 else last).astype(jnp.bfloat16)
            h = group * GROUP + p
            query = jnp.maximum(query_ref[:, h * DH : (h + 1) * DH], 0)
            both_parts = jnp.dot(query, state, preferred_element_type=jnp.float32)
            below = both_parts[:, DH : DH + 1] + EPS_DEN
            attended = both_parts[:, :DH] * (live / below)
            out_ref[:, h * DH : (h + 1) * DH] = attended.astype(jnp.bfloat16)


def attend(core, valid, own, other, query):
    return pl.pallas_call(
        attend_kernel,
        out_shape=jax.ShapeDtypeStruct(query.shape, jnp.bfloat16),
        in_specs=[smem(), smem(), vmem(), vmem(), vmem()],
        out_specs=vmem(),
        scratch_shapes=[pltpu.VMEM((2, ROWS, LANES), jnp.bfloat16)],
        name="attend",
    )(core, valid, own, other, query)


def body(query_in, key_in, value_in, hidden_in, out_weight, norm_gain, temporal_taps, block_valid):
    frames, rows_dev, width_cols, features = query_in.shape
    tokens = frames * rows_dev * width_cols
    core = lax.axis_index("core").astype(jnp.int32).reshape(1)
    swap = [(0, 1), (1, 0)]
    keep, send = local_states(
        core, block_valid, key_in.reshape(tokens, features), value_in.reshape(tokens, features)
    )
    mine = (keep + lax.ppermute(send, "core", swap).astype(jnp.float32)).astype(jnp.bfloat16)
    piece = ROWS // (Z * Y)
    got = lax.all_to_all(mine, ("z", "y"), 0, 0, tiled=True).reshape(Z * Y, piece, LANES)
    prefix, whole = prefixes(got)
    earlier = [
        lax.ppermute(whole, "x", [(i, i + s) for i in range(X - s)]) for s in range(1, X)
    ]
    sums = totals(prefix, *earlier)
    own = lax.all_to_all(sums.reshape(ROWS, LANES), ("z", "y"), 0, 0, tiled=True)
    other = lax.ppermute(own, "core", swap)
    attended = attend(core, block_valid, own, other, query_in.reshape(tokens, features))
    projected = jnp.dot(attended, out_weight, preferred_element_type=jnp.float32)
    residual = (hidden_in.reshape(tokens, features).astype(jnp.float32) + projected).astype(
        jnp.bfloat16
    )
    residual_f = lax.optimization_barrier(residual).astype(jnp.float32)
    inverse = lax.rsqrt(jnp.mean(residual_f * residual_f, axis=-1, keepdims=True) + EPS_NORM)
    normed = (residual_f * inverse * norm_gain).astype(jnp.bfloat16)
    taps = temporal_taps.shape[0]
    tail = normed[tokens - (taps - 1) * rows_dev * width_cols :]
    frames_all = X * Z
    halo = lax.ppermute(tail, ("x", "z"), [(i, i + 1) for i in range(frames_all - 1)])
    extended = jnp.concatenate([halo, normed], axis=0)
    running = jnp.zeros((tokens, features), jnp.float32)
    step = rows_dev * width_cols
    for offset in range(taps):
        lower = (taps - 1 - offset) * step
        running = running + temporal_taps[offset] * extended[lower : lower + tokens].astype(
            jnp.float32
        )
    temporal_f = lax.optimization_barrier(running.astype(jnp.bfloat16)).astype(jnp.float32)
    return (residual_f + temporal_f).astype(jnp.bfloat16).reshape(query_in.shape)


def solution(mesh):
    fine = Mesh(mesh.devices.reshape(X, Z, Y, C), ("x", "z", "y", "core"))
    token = P(("x", "z"), ("y", "core"), None, None)
    placed = (token, token, token, token, P(), P(), P(), P(("x", "z")))
    return jax.shard_map(
        body, mesh=fine, in_specs=placed, out_specs=token, check_vma=False
    )
```

```python
import jax
import jax.numpy as jnp
from jax import lax
from jax.experimental import pallas as pl
from jax.experimental.pallas import tpu as pltpu
from jax.sharding import Mesh, PartitionSpec as P

HEADS = 20
DH = 112
LANES = 128
PIECE = 14
GROUP = HEADS // 2
ROWS = 1024
EPS_DEN = 1e-06
EPS_NORM = 1e-06
X, Z, Y, C = 4, 8, 4, 2
CHUNK = 512


def smem():
    return pl.BlockSpec(memory_space=pltpu.SMEM)


def vmem():
    return pl.BlockSpec(memory_space=pltpu.VMEM)


def limit(mib):
    return pltpu.CompilerParams(vmem_limit_bytes=mib << 20)


def cost(micros):
    return pl.CostEstimate(flops=micros * 1_000_000_000, bytes_accessed=1 << 20, transcendentals=0)


def lane_of(shape):
    return lax.broadcasted_iota(jnp.int32, shape, 1)


def place_of(h):
    return (h * DH) // LANES, (h * DH) % LANES


def free_of(h):
    return ((h + 1) * DH) % LANES


def turn_kernel(valid_ref, key_ref, out_ref):
    tokens, features = key_ref.shape
    row = lax.broadcasted_iota(jnp.int32, (tokens, LANES), 0)
    live = row < valid_ref[0] * 32
    for start in range(0, features, LANES):
        width = min(LANES, features - start)
        keys = jnp.maximum(key_ref[:, start : start + width], 0)
        keys = jnp.where(live[:, :width], keys, jnp.zeros_like(keys))
        out_ref[start : start + width, :] = keys.T


def turn(valid, key):
    tokens, features = key.shape
    return pl.pallas_call(
        turn_kernel,
        out_shape=jax.ShapeDtypeStruct((features, tokens), jnp.bfloat16),
        in_specs=[smem(), vmem()],
        out_specs=vmem(),
        compiler_params=limit(8),
        cost_estimate=cost(4),
        name="turn",
    )(valid, key)


def state_kernel(core_ref, turned, value_ref, keep_ref, send_ref, both):
    tokens, features = value_ref.shape
    lane = lane_of((tokens, LANES))
    one = jnp.ones((tokens, LANES), jnp.bfloat16)

    def values_at(start):
        width = min(LANES, features - start)
        values = value_ref[:, start : start + width]
        if width < LANES:
            values = jnp.concatenate(
                [values, jnp.zeros((tokens, LANES - width), jnp.bfloat16)], axis=1
            )
        return values

    lanes = lane_of((DH, LANES))

    def head(h):
        tile, off = place_of(h)
        keys = turned[h * DH : (h + 1) * DH, :]
        low = values_at(tile * LANES)
        if off == 0:
            low = jnp.where(lane == DH, one, low)
            return jnp.dot(keys, low, preferred_element_type=jnp.float32)
        high = jnp.where(lane == free_of(h), one, values_at((tile + 1) * LANES))
        wide = jnp.dot(
            keys, jnp.concatenate([low, high], axis=1), preferred_element_type=jnp.float32
        )
        return jnp.where(lanes >= off, wide[:, :LANES], wide[:, LANES:])

    for group in range(2):
        slot = (core_ref[0] + group) % 2
        end = group * GROUP + GROUP - 1
        last = head(end)
        for p in range(GROUP - 1):
            h = group * GROUP + p
            free = free_of(h)
            state = head(h)
            if p < 8:
                shift = (free + 2 - place_of(end)[1] - PIECE * p) % LANES
                mask = (lanes >= free + 2) & (lanes < free + 16)
            else:
                shift = (free + 1 - free_of(end)) % LANES
                mask = lanes == free + 1
            moved = pltpu.roll(last, shift, axis=1) if shift else last
            both[slot, p * DH : (p + 1) * DH, :] = jnp.where(mask, moved, state)
        both[slot, (GROUP - 1) * DH :, :] = jnp.zeros((ROWS - (GROUP - 1) * DH, LANES), jnp.float32)
    keep_ref[...] = both[0]
    send_ref[...] = both[1].astype(jnp.bfloat16)


def local_states(core, turned, value):
    return pl.pallas_call(
        state_kernel,
        out_shape=(
            jax.ShapeDtypeStruct((ROWS, LANES), jnp.float32),
            jax.ShapeDtypeStruct((ROWS, LANES), jnp.bfloat16),
        ),
        in_specs=[smem(), vmem(), vmem()],
        out_specs=(vmem(), vmem()),
        scratch_shapes=[pltpu.VMEM((2, ROWS, LANES), jnp.float32)],
        compiler_params=limit(12),
        cost_estimate=cost(4),
        name="local_states",
    )(core, turned, value)


def prefix_kernel(got_ref, prefix_ref, whole_ref):
    total = jnp.zeros(prefix_ref.shape[1:], jnp.float32)
    for z in range(Z):
        for y in range(Y):
            total = total + got_ref[z * Y + y].astype(jnp.float32)
        prefix_ref[z] = total
    for x in range(X):
        whole_ref[x] = total


def prefixes(got):
    piece = got.shape[1:]
    return pl.pallas_call(
        prefix_kernel,
        out_shape=(
            jax.ShapeDtypeStruct((Z,) + piece, jnp.float32),
            jax.ShapeDtypeStruct((X,) + piece, jnp.float32),
        ),
        in_specs=[vmem()],
        out_specs=(vmem(), vmem()),
        compiler_params=limit(4),
        cost_estimate=cost(8),
        name="prefixes",
    )(got)


def totals_kernel(ids_ref, prefix_ref, whole_ref, out_ref):
    before = jnp.zeros(prefix_ref.shape[1:], jnp.float32)
    for x in range(X):
        before = before + jnp.where(x < ids_ref[1], whole_ref[x], 0.0)
    for z in range(Z):
        total = (prefix_ref[z] + before).astype(jnp.bfloat16)
        for y in range(Y):
            out_ref[z * Y + y] = total


def totals(place, prefix, whole):
    piece = prefix.shape[1:]
    return pl.pallas_call(
        totals_kernel,
        out_shape=jax.ShapeDtypeStruct((Z * Y,) + piece, jnp.bfloat16),
        in_specs=[smem(), vmem(), vmem()],
        out_specs=vmem(),
        compiler_params=limit(4),
        cost_estimate=cost(8),
        name="totals",
    )(place, prefix, whole)


def mix_kernel(
    core_ref,
    valid_ref,
    own_ref,
    other_ref,
    query_ref,
    hidden_ref,
    gain_ref,
    weight,
    residual,
    normed_ref,
    tail_ref,
    states,
    attended,
):
    tokens, features = query_ref.shape
    tail = tail_ref.shape[0]
    step = tokens // 4
    own = core_ref[0]
    states[own] = own_ref[...]
    states[1 - own] = other_ref[...]
    lanes = lane_of((DH, LANES))
    zero = jnp.zeros((DH, LANES), jnp.bfloat16)

    def unpack(group):
        packed = [states[group, p * DH : (p + 1) * DH, :] for p in range(GROUP - 1)]
        end = group * GROUP + GROUP - 1
        off = place_of(end)[1]
        last = jnp.zeros((DH, LANES), jnp.float32)
        for p in range(GROUP - 1):
            free = free_of(group * GROUP + p)
            if p < 8:
                shift = (off + PIECE * p - free - 2) % LANES
                first = (off + PIECE * p) % LANES
                mask = (lanes >= first) & (lanes < first + PIECE)
                if first + PIECE > LANES:
                    mask = mask | (lanes < first + PIECE - LANES)
            else:
                shift = (free_of(end) - free - 1) % LANES
                mask = lanes == free_of(end)
            wide = packed[p].astype(jnp.float32)
            moved = pltpu.roll(wide, shift, axis=1) if shift else wide
            last = jnp.where(mask, moved, last)
        return packed + [last.astype(jnp.bfloat16)]

    def window(h, packed):
        off = place_of(h)[1]
        if off == 0:
            wide = jnp.where(lanes <= DH, packed, zero)
        else:
            low = jnp.where(lanes >= off, packed, zero)
            high = jnp.where(lanes <= off - 16, packed, zero)
            wide = jnp.concatenate([low, high], axis=1)
        return wide

    lane = lane_of((tokens, LANES))
    row = lax.broadcasted_iota(jnp.int32, (tokens, 1), 0)
    live = (row < valid_ref[0] * step).astype(jnp.float32)
    carry = None
    for group in range(2):
        unpacked = unpack(group)
        for p in range(GROUP):
            h = group * GROUP + p
            tile, off = place_of(h)
            start = tile * LANES
            stop = min(start + (LANES if off == 0 else 2 * LANES), features)
            wide = window(h, unpacked[p])
            parts = []
            if off:
                parts.append(jnp.zeros((off, wide.shape[1]), jnp.bfloat16))
            parts.append(wide)
            rest = stop - start - off - DH
            if rest:
                parts.append(jnp.zeros((rest, wide.shape[1]), jnp.bfloat16))
            matrix = jnp.concatenate(parts, axis=0) if len(parts) > 1 else wide
            query = jnp.maximum(query_ref[:, start:stop], 0)
            got = jnp.dot(query, matrix, preferred_element_type=jnp.float32)
            below = got[:, off + DH : off + DH + 1] + EPS_DEN
            scale = jnp.broadcast_to(live / below, (tokens, LANES))
            low = got[:, :LANES] * scale
            if off == 0:
                carry = low
                continue
            full = jnp.where(lane >= off, low, carry)
            attended[:, start : start + LANES] = full.astype(jnp.bfloat16)
            carry = got[:, LANES:] * scale
    left = features - (features // LANES) * LANES
    if left:
        attended[:, features - left :] = carry[:, :left].astype(jnp.bfloat16)

    squares = jnp.zeros((tokens, LANES), jnp.float32)
    for s in range(0, features, CHUNK):
        w = min(CHUNK, features - s)
        projected = jnp.dot(
            attended[...], weight[:, s : s + w], preferred_element_type=jnp.float32
        )
        rounded = (hidden_ref[:, s : s + w].astype(jnp.float32) + projected).astype(jnp.bfloat16)
        residual[:, s : s + w] = rounded
        wide = rounded.astype(jnp.float32)
        wide = wide * wide
        for a in range(0, w, LANES):
            b = min(LANES, w - a)
            part = wide[:, a : a + b]
            if b < LANES:
                part = jnp.concatenate([part, jnp.zeros((tokens, LANES - b), jnp.float32)], axis=1)
            squares = squares + part
    mean = jnp.sum(squares, axis=1, keepdims=True) / features
    inverse = jnp.broadcast_to(lax.rsqrt(mean + EPS_NORM), (tokens, LANES))
    for s in range(0, features, LANES):
        w = min(LANES, features - s)
        here = residual[:, s : s + w].astype(jnp.float32)
        normed = (here * inverse[:, :w] * gain_ref[:, s : s + w]).astype(jnp.bfloat16)
        normed_ref[:, s : s + w] = normed
        tail_ref[:, s : s + w] = normed[tokens - tail :]


def mix(core, valid, own, other, query, hidden, gain, weight):
    tokens, features = query.shape
    full = jax.ShapeDtypeStruct((tokens, features), jnp.bfloat16)
    return pl.pallas_call(
        mix_kernel,
        out_shape=(full, full, jax.ShapeDtypeStruct((tokens // 2, features), jnp.bfloat16)),
        in_specs=[smem(), smem()] + [vmem()] * 6,
        out_specs=(vmem(), vmem(), vmem()),
        scratch_shapes=[
            pltpu.VMEM((2, ROWS, LANES), jnp.bfloat16),
            pltpu.VMEM((tokens, features), jnp.bfloat16),
        ],
        compiler_params=limit(24),
        cost_estimate=cost(6),
        name="mix",
    )(core, valid, own, other, query, hidden, gain, weight)


def temporal_kernel(residual_ref, normed_ref, halo_ref, taps_ref, out_ref):
    tokens, features = residual_ref.shape
    tail = halo_ref.shape[0]
    step = tokens // 4
    for s in range(0, features, LANES):
        w = min(LANES, features - s)
        normed = jnp.concatenate([halo_ref[:, s : s + w], normed_ref[:, s : s + w]], axis=0)
        normed = normed.astype(jnp.float32)
        total = jnp.zeros((tokens, w), jnp.float32)
        for offset in range(3):
            lower = tail - offset * step
            total = total + taps_ref[offset : offset + 1, s : s + w] * normed[lower : lower + tokens]
        temporal = total.astype(jnp.bfloat16).astype(jnp.float32)
        here = residual_ref[:, s : s + w].astype(jnp.float32)
        out_ref[:, s : s + w] = (here + temporal).astype(jnp.bfloat16)


def temporal_mix(residual, normed, halo, taps):
    return pl.pallas_call(
        temporal_kernel,
        out_shape=jax.ShapeDtypeStruct(residual.shape, jnp.bfloat16),
        in_specs=[vmem()] * 4,
        out_specs=vmem(),
        compiler_params=limit(8),
        cost_estimate=cost(1),
        name="temporal_mix",
    )(residual, normed, halo, taps)


def body(query_in, key_in, value_in, hidden_in, out_weight, norm_gain, temporal_taps, block_valid):
    frames, rows_dev, width_cols, features = query_in.shape
    tokens = frames * rows_dev * width_cols
    ids = jnp.stack([lax.axis_index("core"), lax.axis_index("x")]).astype(jnp.int32)
    query = query_in.reshape(tokens, features)
    hidden = hidden_in.reshape(tokens, features)
    swap = [(0, 1), (1, 0)]
    keys = turn(block_valid, key_in.reshape(tokens, features))
    keep, send = local_states(ids, keys, value_in.reshape(tokens, features))
    fetched = lax.ppermute(send, "core", swap)
    mine = (keep + fetched.astype(jnp.float32)).astype(jnp.bfloat16)
    piece = ROWS // (Z * Y)
    with jax.named_scope("scatter"):
        got = lax.all_to_all(mine, ("z", "y"), 0, 0, tiled=True).reshape(Z * Y, piece, LANES)
    prefix, whole = prefixes(got)
    wholes = lax.all_to_all(whole, "x", 0, 0, tiled=True)
    with jax.named_scope("gather"):
        own = lax.all_to_all(totals(ids, prefix, wholes), ("z", "y"), 0, 0, tiled=True)
    own = own.reshape(ROWS, LANES)
    other = lax.ppermute(own, "core", swap)
    residual, normed, tail = mix(
        ids, block_valid, own, other, query, hidden, norm_gain.reshape(1, features), out_weight
    )
    halo = lax.ppermute(tail, ("x", "z"), [(i, i + 1) for i in range(X * Z - 1)])
    return temporal_mix(residual, normed, halo, temporal_taps).reshape(query_in.shape)


def solution(mesh):
    fine = Mesh(mesh.devices.reshape(X, Z, Y, C), ("x", "z", "y", "core"))
    token = P(("x", "z"), ("y", "core"), None, None)
    placed = (token, token, token, token, P(), P(), P(), P(("x", "z")))
    return jax.shard_map(
        body, mesh=fine, in_specs=placed, out_specs=token, check_vma=False
    )
```

```python
import functools

import jax
import jax.numpy as jnp
from jax import lax
from jax.experimental import pallas as pl
from jax.experimental.pallas import tpu as pltpu
from jax.sharding import Mesh, PartitionSpec as P


HEADS = 20
DH = 112
LANES = 128
PIECE = 14
GROUP = HEADS // 2
ROWS = 1024
EPS_DEN = 1e-06
EPS_NORM = 1e-06
X, Z, Y, C = 4, 8, 4, 2
CHUNK = 512


def smem():
    return pl.BlockSpec(memory_space=pltpu.SMEM)


def vmem():
    return pl.BlockSpec(memory_space=pltpu.VMEM)


def limit(mib):
    return pltpu.CompilerParams(vmem_limit_bytes=mib << 20)


def cost(micros):
    return pl.CostEstimate(flops=micros * 1_000_000_000, bytes_accessed=1 << 20, transcendentals=0)


def lane_of(shape):
    return lax.broadcasted_iota(jnp.int32, shape, 1)


def place_of(h):
    return (h * DH) // LANES, (h * DH) % LANES


def free_of(h):
    return ((h + 1) * DH) % LANES


def turn_kernel(valid_ref, key_ref, out_ref):
    tokens, features = key_ref.shape
    row = lax.broadcasted_iota(jnp.int32, (tokens, LANES), 0)
    live = row < valid_ref[0] * 32
    for start in range(0, features, LANES):
        width = min(LANES, features - start)
        keys = jnp.maximum(key_ref[:, start : start + width], 0)
        keys = jnp.where(live[:, :width], keys, jnp.zeros_like(keys))
        out_ref[start : start + width, :] = keys.T


def turn(valid, key):
    tokens, features = key.shape
    return pl.pallas_call(
        turn_kernel,
        out_shape=jax.ShapeDtypeStruct((features, tokens), jnp.bfloat16),
        in_specs=[smem(), vmem()],
        out_specs=vmem(),
        compiler_params=limit(8),
        cost_estimate=cost(4),
        name="turn",
    )(valid, key)


def group_states(group, turned, value_ref, out_ref):
    tokens, features = value_ref.shape
    lane = lane_of((tokens, LANES))
    one = jnp.ones((tokens, LANES), jnp.bfloat16)
    lanes = lane_of((DH, LANES))

    def values_at(start):
        width = min(LANES, features - start)
        values = value_ref[:, start : start + width]
        if width < LANES:
            values = jnp.concatenate(
                [values, jnp.zeros((tokens, LANES - width), jnp.bfloat16)], axis=1
            )
        return values

    def head(h):
        tile, off = place_of(h)
        keys = turned[h * DH : (h + 1) * DH, :]
        low = values_at(tile * LANES)
        if off == 0:
            low = jnp.where(lane == DH, one, low)
            return jnp.dot(keys, low, preferred_element_type=jnp.float32)
        high = jnp.where(lane == free_of(h), one, values_at((tile + 1) * LANES))
        wide = jnp.dot(
            keys, jnp.concatenate([low, high], axis=1), preferred_element_type=jnp.float32
        )
        return jnp.where(lanes >= off, wide[:, :LANES], wide[:, LANES:])

    end = group * GROUP + GROUP - 1
    last = head(end)
    for p in range(GROUP - 1):
        h = group * GROUP + p
        free = free_of(h)
        state = head(h)
        if p < 8:
            shift = (free + 2 - place_of(end)[1] - PIECE * p) % LANES
            mask = (lanes >= free + 2) & (lanes < free + 16)
        else:
            shift = (free + 1 - free_of(end)) % LANES
            mask = lanes == free + 1
        moved = pltpu.roll(last, shift, axis=1) if shift else last
        state = jnp.where(mask, moved, state)
        out_ref[p * DH : (p + 1) * DH, :] = state.astype(out_ref.dtype)
    rest = ROWS - (GROUP - 1) * DH
    out_ref[(GROUP - 1) * DH :, :] = jnp.zeros((rest, LANES), out_ref.dtype)


def state_kernel(mine, ids_ref, turned, value_ref, out_ref):
    for group in range(2):

        @pl.when(ids_ref[0] == (group if mine else 1 - group))
        def _():
            group_states(group, turned, value_ref, out_ref)


def local_states(ids, turned, value, mine):
    return pl.pallas_call(
        functools.partial(state_kernel, mine),
        out_shape=jax.ShapeDtypeStruct((ROWS, LANES), jnp.float32 if mine else jnp.bfloat16),
        in_specs=[smem(), vmem(), vmem()],
        out_specs=vmem(),
        compiler_params=limit(12),
        cost_estimate=cost(1),
        name="kept_states" if mine else "sent_states",
    )(ids, turned, value)


def prefix_kernel(got_ref, prefix_ref, whole_ref):
    total = jnp.zeros(prefix_ref.shape[1:], jnp.float32)
    for z in range(Z):
        for y in range(Y):
            total = total + got_ref[z * Y + y].astype(jnp.float32)
        prefix_ref[z] = total
    for x in range(X):
        whole_ref[x] = total


def prefixes(got):
    piece = got.shape[1:]
    return pl.pallas_call(
        prefix_kernel,
        out_shape=(
            jax.ShapeDtypeStruct((Z,) + piece, jnp.float32),
            jax.ShapeDtypeStruct((X,) + piece, jnp.float32),
        ),
        in_specs=[vmem()],
        out_specs=(vmem(), vmem()),
        compiler_params=limit(4),
        cost_estimate=cost(8),
        name="prefixes",
    )(got)


def totals_kernel(ids_ref, prefix_ref, whole_ref, out_ref):
    before = jnp.zeros(prefix_ref.shape[1:], jnp.float32)
    for x in range(X):
        before = before + jnp.where(x < ids_ref[1], whole_ref[x], 0.0)
    for z in range(Z):
        total = (prefix_ref[z] + before).astype(jnp.bfloat16)
        for y in range(Y):
            out_ref[z * Y + y] = total


def totals(place, prefix, whole):
    piece = prefix.shape[1:]
    return pl.pallas_call(
        totals_kernel,
        out_shape=jax.ShapeDtypeStruct((Z * Y,) + piece, jnp.bfloat16),
        in_specs=[smem(), vmem(), vmem()],
        out_specs=vmem(),
        compiler_params=limit(4),
        cost_estimate=cost(8),
        name="totals",
    )(place, prefix, whole)


def project(
    ids_ref, valid_ref, own_ref, other_ref, query_ref, hidden_ref, gain_ref, weight, first, attended, residual, normed_ref
):
    count, features = query_ref.shape
    step = count // 2
    own = ids_ref[0]
    lanes = lane_of((DH, LANES))
    zero = jnp.zeros((DH, LANES), jnp.bfloat16)

    def stored(group, p):
        at = slice(p * DH, (p + 1) * DH)
        return jnp.where(own == group, own_ref[at, :], other_ref[at, :])

    def unpack(group):
        packed = [stored(group, p) for p in range(GROUP - 1)]
        end = group * GROUP + GROUP - 1
        off = place_of(end)[1]
        last = jnp.zeros((DH, LANES), jnp.float32)
        for p in range(GROUP - 1):
            free = free_of(group * GROUP + p)
            if p < 8:
                shift = (off + PIECE * p - free - 2) % LANES
                start = (off + PIECE * p) % LANES
                mask = (lanes >= start) & (lanes < start + PIECE)
                if start + PIECE > LANES:
                    mask = mask | (lanes < start + PIECE - LANES)
            else:
                shift = (free_of(end) - free - 1) % LANES
                mask = lanes == free_of(end)
            wide = packed[p].astype(jnp.float32)
            moved = pltpu.roll(wide, shift, axis=1) if shift else wide
            last = jnp.where(mask, moved, last)
        return packed + [last.astype(jnp.bfloat16)]

    def window(h, packed):
        off = place_of(h)[1]
        if off == 0:
            return jnp.where(lanes <= DH, packed, zero)
        low = jnp.where(lanes >= off, packed, zero)
        high = jnp.where(lanes <= off - 16, packed, zero)
        return jnp.concatenate([low, high], axis=1)

    row = lax.broadcasted_iota(jnp.int32, (count, 1), 0)
    live = (row + first * step < valid_ref[0] * step).astype(jnp.float32)
    lane = lane_of((count, LANES))
    carry = None
    for group in range(2):
        unpacked = unpack(group)
        for p in range(GROUP):
            h = group * GROUP + p
            tile, off = place_of(h)
            start = tile * LANES
            stop = min(start + (LANES if off == 0 else 2 * LANES), features)
            wide = window(h, unpacked[p])
            parts = [wide]
            if off:
                parts.insert(0, jnp.zeros((off, wide.shape[1]), jnp.bfloat16))
            rest = stop - start - off - DH
            if rest:
                parts.append(jnp.zeros((rest, wide.shape[1]), jnp.bfloat16))
            matrix = jnp.concatenate(parts, axis=0) if len(parts) > 1 else wide
            query = jnp.maximum(query_ref[:, start:stop], 0)
            got = jnp.dot(query, matrix, preferred_element_type=jnp.float32)
            below = got[:, off + DH : off + DH + 1] + EPS_DEN
            scale = jnp.broadcast_to(live / below, (count, LANES))
            low = got[:, :LANES] * scale
            if off == 0:
                carry = low
                continue
            full = jnp.where(lane >= off, low, carry)
            attended[:, start : start + LANES] = full.astype(jnp.bfloat16)
            carry = got[:, LANES:] * scale
    left = features % LANES
    if left:
        attended[:, features - left :] = carry[:, :left].astype(jnp.bfloat16)

    squares = jnp.zeros((count, LANES), jnp.float32)
    for s in range(0, features, CHUNK):
        w = min(CHUNK, features - s)
        projected = jnp.dot(
            attended[...], weight[:, s : s + w], preferred_element_type=jnp.float32
        )
        rounded = (hidden_ref[:, s : s + w].astype(jnp.float32) + projected).astype(jnp.bfloat16)
        residual[:, s : s + w] = rounded
        wide = rounded.astype(jnp.float32)
        wide = wide * wide
        for a in range(0, w, LANES):
            b = min(LANES, w - a)
            part = wide[:, a : a + b]
            if b < LANES:
                part = jnp.concatenate([part, jnp.zeros((count, LANES - b), jnp.float32)], axis=1)
            squares = squares + part
    mean = jnp.sum(squares, axis=1, keepdims=True) / features
    inverse = jnp.broadcast_to(lax.rsqrt(mean + EPS_NORM), (count, LANES))
    for s in range(0, features, LANES):
        w = min(LANES, features - s)
        here = residual[:, s : s + w].astype(jnp.float32)
        normed = (here * inverse[:, :w] * gain_ref[:, s : s + w]).astype(jnp.bfloat16)
        normed_ref[:, s : s + w] = normed


def tail_kernel(ids_ref, valid_ref, own_ref, other_ref, query_ref, hidden_ref, gain_ref, weight, residual, normed_ref, attended):
    half = query_ref.shape[0] // 2
    project(
        ids_ref, valid_ref, own_ref, other_ref, query_ref.at[half:, :], hidden_ref.at[half:, :],
        gain_ref, weight, 2, attended, residual, normed_ref,
    )


def tail_of(ids, valid, own, other, query, hidden, gain, weight):
    tokens, features = query.shape
    half = jax.ShapeDtypeStruct((tokens // 2, features), jnp.bfloat16)
    return pl.pallas_call(
        tail_kernel,
        out_shape=(half, half),
        in_specs=[smem(), smem()] + [vmem()] * 6,
        out_specs=(vmem(), vmem()),
        scratch_shapes=[pltpu.VMEM(half.shape, jnp.bfloat16)],
        compiler_params=limit(24),
        cost_estimate=cost(3),
        name="tail_of",
    )(ids, valid, own, other, query, hidden, gain, weight)


def head_kernel(
    ids_ref, valid_ref, own_ref, other_ref, query_ref, hidden_ref, gain_ref, weight,
    tail_residual, tail_normed, taps_ref, out_ref, residual, partial_ref, attended, normed_ref
):
    count, features = residual.shape
    step = count // 2
    project(
        ids_ref, valid_ref, own_ref, other_ref, query_ref.at[:count, :], hidden_ref.at[:count, :],
        gain_ref, weight, 0, attended, residual, normed_ref,
    )
    for s in range(0, features, LANES):
        w = min(LANES, features - s)
        taps = [taps_ref[j : j + 1, s : s + w] for j in range(3)]
        frames = [
            ref[t * step : (t + 1) * step, s : s + w].astype(jnp.float32)
            for ref in (normed_ref, tail_normed)
            for t in range(2)
        ]
        partial_ref[:step, s : s + w] = taps[0] * frames[0]
        partial_ref[step:, s : s + w] = taps[0] * frames[1] + taps[1] * frames[0]
        for t in range(2):
            total = taps[0] * frames[t + 2] + taps[1] * frames[t + 1] + taps[2] * frames[t]
            temporal = total.astype(jnp.bfloat16).astype(jnp.float32)
            at = slice(t * step, (t + 1) * step)
            here = tail_residual[at, s : s + w].astype(jnp.float32)
            out_ref[at, s : s + w] = (here + temporal).astype(jnp.bfloat16)


def head_of(ids, valid, own, other, query, hidden, gain, weight, tail_residual, tail_normed, taps):
    tokens, features = query.shape
    half = (tokens // 2, features)
    return pl.pallas_call(
        head_kernel,
        grid=(1,),
        out_shape=(
            jax.ShapeDtypeStruct(query.shape, jnp.bfloat16),
            jax.ShapeDtypeStruct(half, jnp.bfloat16),
            jax.ShapeDtypeStruct(half, jnp.float32),
        ),
        in_specs=[smem(), smem()] + [vmem()] * 9,
        out_specs=(pl.BlockSpec(half, lambda i: (1, 0)), vmem(), vmem()),
        scratch_shapes=[pltpu.VMEM(half, jnp.bfloat16), pltpu.VMEM(half, jnp.bfloat16)],
        compiler_params=limit(24),
        cost_estimate=cost(3),
        name="head_of",
    )(ids, valid, own, other, query, hidden, gain, weight, tail_residual, tail_normed, taps)


def finish_kernel(unused_ref, residual_ref, partial_ref, halo_ref, taps_ref, out_ref):
    count, features = residual_ref.shape
    step = count // 2
    for s in range(0, features, LANES):
        w = min(LANES, features - s)
        taps = [taps_ref[j : j + 1, s : s + w] for j in range(3)]
        oldest = halo_ref[:step, s : s + w].astype(jnp.float32)
        older = halo_ref[step:, s : s + w].astype(jnp.float32)
        totals = [
            partial_ref[:step, s : s + w] + taps[1] * older + taps[2] * oldest,
            partial_ref[step:, s : s + w] + taps[2] * older,
        ]
        for t, total in enumerate(totals):
            temporal = total.astype(jnp.bfloat16).astype(jnp.float32)
            at = slice(t * step, (t + 1) * step)
            here = residual_ref[at, s : s + w].astype(jnp.float32)
            out_ref[at, s : s + w] = (here + temporal).astype(jnp.bfloat16)


def finish(out, residual, partial, halo, taps):
    return pl.pallas_call(
        finish_kernel,
        grid=(1,),
        out_shape=jax.ShapeDtypeStruct(out.shape, out.dtype),
        in_specs=[pl.BlockSpec(memory_space=pl.ANY)] + [vmem()] * 4,
        out_specs=pl.BlockSpec(residual.shape, lambda i: (0, 0)),
        input_output_aliases={0: 0},
        compiler_params=limit(8),
        cost_estimate=cost(1),
        name="finish",
    )(out, residual, partial, halo, taps)


def body(query_in, key_in, value_in, hidden_in, out_weight, norm_gain, temporal_taps, block_valid):
    frames, rows_dev, width_cols, features = query_in.shape
    tokens = frames * rows_dev * width_cols
    ids = jnp.stack([lax.axis_index("core"), lax.axis_index("x")]).astype(jnp.int32)
    query = query_in.reshape(tokens, features)
    hidden = hidden_in.reshape(tokens, features)
    swap = [(0, 1), (1, 0)]
    keys = turn(block_valid, key_in.reshape(tokens, features))
    value = value_in.reshape(tokens, features)
    send = local_states(ids, keys, value, False)
    fetched = lax.ppermute(send, "core", swap)
    keep = local_states(ids, keys, value, True)
    mine = (keep + fetched.astype(jnp.float32)).astype(jnp.bfloat16)
    piece = ROWS // (Z * Y)
    got = lax.all_to_all(mine, ("z", "y"), 0, 0, tiled=True).reshape(Z * Y, piece, LANES)
    prefix, whole = prefixes(got)
    wholes = lax.all_to_all(whole, "x", 0, 0, tiled=True)
    own = lax.all_to_all(totals(ids, prefix, wholes), ("z", "y"), 0, 0, tiled=True)
    own = own.reshape(ROWS, LANES)
    other = lax.ppermute(own, "core", swap)
    gain = norm_gain.reshape(1, features)
    shared = (ids, block_valid, own, other, query, hidden, gain, out_weight)
    tail_residual, tail_normed = tail_of(*shared)
    halo = lax.ppermute(tail_normed, ("x", "z"), [(i, i + 1) for i in range(X * Z - 1)])
    out, residual, partial = head_of(*shared, tail_residual, tail_normed, temporal_taps)
    mixed = finish(out, residual, partial, halo, temporal_taps)
    return mixed.reshape(query_in.shape)


def solution(mesh):
    fine = Mesh(mesh.devices.reshape(X, Z, Y, C), ("x", "z", "y", "core"))
    token = P(("x", "z"), ("y", "core"), None, None)
    placed = (token, token, token, token, P(), P(), P(), P(("x", "z")))

    return jax.shard_map(body, mesh=fine, in_specs=placed, out_specs=token, check_vma=False)
```

```python
import functools

import jax
import jax.numpy as jnp
from jax import lax
from jax.experimental import pallas as pl
from jax.experimental.pallas import tpu as pltpu
from jax.sharding import Mesh, PartitionSpec as P


HEADS = 20
DH = 112
LANES = 128
PIECE = 14
GROUP = HEADS // 2
ROWS = 1024
EPS_DEN = 1e-06
EPS_NORM = 1e-06
X, Z, Y, C = 4, 8, 4, 2
CHUNK = 512


def smem():
    return pl.BlockSpec(memory_space=pltpu.SMEM)


def vmem():
    return pl.BlockSpec(memory_space=pltpu.VMEM)


def limit(mib):
    return pltpu.CompilerParams(vmem_limit_bytes=mib << 20)


def cost(micros):
    return pl.CostEstimate(flops=micros * 1_000_000_000, bytes_accessed=1 << 20, transcendentals=0)


def lane_of(shape):
    return lax.broadcasted_iota(jnp.int32, shape, 1)


def place_of(h):
    return (h * DH) // LANES, (h * DH) % LANES


def free_of(h):
    return ((h + 1) * DH) % LANES


def group_states(group, turned, value_ref, out_ref):
    tokens, features = value_ref.shape
    lane = lane_of((tokens, LANES))
    one = jnp.ones((tokens, LANES), jnp.bfloat16)
    lanes = lane_of((DH, LANES))

    def values_at(start):
        width = min(LANES, features - start)
        values = value_ref[:, start : start + width]
        if width < LANES:
            values = jnp.concatenate(
                [values, jnp.zeros((tokens, LANES - width), jnp.bfloat16)], axis=1
            )
        return values

    def head(h):
        tile, off = place_of(h)
        keys = turned[h * DH : (h + 1) * DH, :]
        low = values_at(tile * LANES)
        if off == 0:
            low = jnp.where(lane == DH, one, low)
            return jnp.dot(keys, low, preferred_element_type=jnp.float32)
        high = jnp.where(lane == free_of(h), one, values_at((tile + 1) * LANES))
        wide = jnp.dot(
            keys, jnp.concatenate([low, high], axis=1), preferred_element_type=jnp.float32
        )
        return jnp.where(lanes >= off, wide[:, :LANES], wide[:, LANES:])

    end = group * GROUP + GROUP - 1
    last = head(end)
    for p in range(GROUP - 1):
        h = group * GROUP + p
        free = free_of(h)
        state = head(h)
        if p < 8:
            shift = (free + 2 - place_of(end)[1] - PIECE * p) % LANES
            mask = (lanes >= free + 2) & (lanes < free + 16)
        else:
            shift = (free + 1 - free_of(end)) % LANES
            mask = lanes == free + 1
        moved = pltpu.roll(last, shift, axis=1) if shift else last
        state = jnp.where(mask, moved, state)
        out_ref[p * DH : (p + 1) * DH, :] = state.astype(out_ref.dtype)
    rest = ROWS - (GROUP - 1) * DH
    out_ref[(GROUP - 1) * DH :, :] = jnp.zeros((rest, LANES), out_ref.dtype)


def live_kernel(valid_ref, out_ref):
    tokens = out_ref.shape[0]
    row = lax.broadcasted_iota(jnp.int32, out_ref.shape, 0)
    live = row < valid_ref[0] * (tokens // 4)
    out_ref[...] = jnp.where(live, 1.0, 0.0).astype(jnp.bfloat16)


def live_of(valid, tokens):
    return pl.pallas_call(
        live_kernel,
        out_shape=jax.ShapeDtypeStruct((tokens, LANES), jnp.bfloat16),
        in_specs=[smem()],
        out_specs=vmem(),
        compiler_params=limit(2),
        cost_estimate=cost(8),
        name="live_of",
    )(valid)


def turn_kernel(live_ref, key_ref, out_ref):
    _, features = key_ref.shape
    live = live_ref[...]
    for start in range(0, features, LANES):
        width = min(LANES, features - start)
        keys = jnp.maximum(key_ref[:, start : start + width], 0) * live[:, :width]
        out_ref[start : start + width, :] = keys.T


def turn(live, key):
    tokens, features = key.shape
    return pl.pallas_call(
        turn_kernel,
        out_shape=jax.ShapeDtypeStruct((features, tokens), jnp.bfloat16),
        in_specs=[vmem(), vmem()],
        out_specs=vmem(),
        compiler_params=limit(8),
        name="turn",
    )(live, key)


def state_kernel(mine, turned, value_ref, out_ref):
    core = lax.axis_index("core")
    for group in range(2):

        @pl.when(core == (group if mine else 1 - group))
        def _():
            group_states(group, turned, value_ref, out_ref)


def local_states(turned, value, mine):
    return pl.pallas_call(
        functools.partial(state_kernel, mine),
        out_shape=jax.ShapeDtypeStruct((ROWS, LANES), jnp.float32 if mine else jnp.bfloat16),
        in_specs=[vmem(), vmem()],
        out_specs=vmem(),
        compiler_params=limit(8),
        cost_estimate=cost(1),
        name="kept_states" if mine else "sent_states",
    )(turned, value)


def prefix_kernel(got_ref, prefix_ref, whole_ref):
    total = jnp.zeros(prefix_ref.shape[1:], jnp.float32)
    for z in range(Z):
        for y in range(Y):
            total = total + got_ref[z * Y + y].astype(jnp.float32)
        prefix_ref[z] = total
    for x in range(X):
        whole_ref[x] = total


def prefixes(got):
    piece = got.shape[1:]
    return pl.pallas_call(
        prefix_kernel,
        out_shape=(
            jax.ShapeDtypeStruct((Z,) + piece, jnp.float32),
            jax.ShapeDtypeStruct((X,) + piece, jnp.float32),
        ),
        in_specs=[vmem()],
        out_specs=(vmem(), vmem()),
        compiler_params=limit(4),
        cost_estimate=cost(8),
        name="prefixes",
    )(got)


def totals_kernel(prefix_ref, whole_ref, out_ref):
    place = lax.axis_index("x")
    before = jnp.zeros(prefix_ref.shape[1:], jnp.float32)
    for x in range(X):
        before = before + jnp.where(x < place, whole_ref[x], 0.0)
    for z in range(Z):
        total = (prefix_ref[z] + before).astype(jnp.bfloat16)
        for y in range(Y):
            out_ref[z * Y + y] = total


def totals(prefix, whole):
    piece = prefix.shape[1:]
    return pl.pallas_call(
        totals_kernel,
        out_shape=jax.ShapeDtypeStruct((Z * Y,) + piece, jnp.bfloat16),
        in_specs=[vmem(), vmem()],
        out_specs=vmem(),
        compiler_params=limit(4),
        cost_estimate=cost(8),
        name="totals",
    )(prefix, whole)


def project(
    valid_ref, own_ref, other_ref, query_ref, hidden_ref, gain_ref, weight, first, attended, residual, normed_ref
):
    count, features = query_ref.shape
    step = count // 2
    own = lax.axis_index("core")
    lanes = lane_of((DH, LANES))
    zero = jnp.zeros((DH, LANES), jnp.bfloat16)

    def stored(group, p):
        at = slice(p * DH, (p + 1) * DH)
        return jnp.where(own == group, own_ref[at, :], other_ref[at, :])

    def unpack(group):
        packed = [stored(group, p) for p in range(GROUP - 1)]
        end = group * GROUP + GROUP - 1
        off = place_of(end)[1]
        last = jnp.zeros((DH, LANES), jnp.float32)
        for p in range(GROUP - 1):
            free = free_of(group * GROUP + p)
            if p < 8:
                shift = (off + PIECE * p - free - 2) % LANES
                start = (off + PIECE * p) % LANES
                mask = (lanes >= start) & (lanes < start + PIECE)
                if start + PIECE > LANES:
                    mask = mask | (lanes < start + PIECE - LANES)
            else:
                shift = (free_of(end) - free - 1) % LANES
                mask = lanes == free_of(end)
            wide = packed[p].astype(jnp.float32)
            moved = pltpu.roll(wide, shift, axis=1) if shift else wide
            last = jnp.where(mask, moved, last)
        return packed + [last.astype(jnp.bfloat16)]

    def window(h, packed):
        off = place_of(h)[1]
        if off == 0:
            return jnp.where(lanes <= DH, packed, zero)
        low = jnp.where(lanes >= off, packed, zero)
        high = jnp.where(lanes <= off - 16, packed, zero)
        return jnp.concatenate([low, high], axis=1)

    row = lax.broadcasted_iota(jnp.int32, (count, 1), 0)
    live = (row + first * step < valid_ref[0] * step).astype(jnp.float32)
    lane = lane_of((count, LANES))
    carry = None
    for group in range(2):
        unpacked = unpack(group)
        for p in range(GROUP):
            h = group * GROUP + p
            tile, off = place_of(h)
            start = tile * LANES
            stop = min(start + (LANES if off == 0 else 2 * LANES), features)
            wide = window(h, unpacked[p])
            parts = [wide]
            if off:
                parts.insert(0, jnp.zeros((off, wide.shape[1]), jnp.bfloat16))
            rest = stop - start - off - DH
            if rest:
                parts.append(jnp.zeros((rest, wide.shape[1]), jnp.bfloat16))
            matrix = jnp.concatenate(parts, axis=0) if len(parts) > 1 else wide
            query = jnp.maximum(query_ref[:, start:stop], 0)
            got = jnp.dot(query, matrix, preferred_element_type=jnp.float32)
            below = got[:, off + DH : off + DH + 1] + EPS_DEN
            scale = jnp.broadcast_to(live / below, (count, LANES))
            low = got[:, :LANES] * scale
            if off == 0:
                carry = low
                continue
            full = jnp.where(lane >= off, low, carry)
            attended[:, start : start + LANES] = full.astype(jnp.bfloat16)
            carry = got[:, LANES:] * scale
    left = features % LANES
    if left:
        attended[:, features - left :] = carry[:, :left].astype(jnp.bfloat16)

    squares = jnp.zeros((count, LANES), jnp.float32)
    for s in range(0, features, CHUNK):
        w = min(CHUNK, features - s)
        projected = jnp.dot(
            attended[...], weight[:, s : s + w], preferred_element_type=jnp.float32
        )
        rounded = (hidden_ref[:, s : s + w].astype(jnp.float32) + projected).astype(jnp.bfloat16)
        residual[:, s : s + w] = rounded
        wide = rounded.astype(jnp.float32)
        wide = wide * wide
        for a in range(0, w, LANES):
            b = min(LANES, w - a)
            part = wide[:, a : a + b]
            if b < LANES:
                part = jnp.concatenate([part, jnp.zeros((count, LANES - b), jnp.float32)], axis=1)
            squares = squares + part
    mean = jnp.sum(squares, axis=1, keepdims=True) / features
    inverse = jnp.broadcast_to(lax.rsqrt(mean + EPS_NORM), (count, LANES))
    for s in range(0, features, LANES):
        w = min(LANES, features - s)
        here = residual[:, s : s + w].astype(jnp.float32)
        normed = (here * inverse[:, :w] * gain_ref[:, s : s + w]).astype(jnp.bfloat16)
        normed_ref[:, s : s + w] = normed


def tail_kernel(valid_ref, own_ref, other_ref, query_ref, hidden_ref, gain_ref, weight, residual, normed_ref, attended):
    half = query_ref.shape[0] // 2
    project(
        valid_ref, own_ref, other_ref, query_ref.at[half:, :], hidden_ref.at[half:, :],
        gain_ref, weight, 2, attended, residual, normed_ref,
    )


def tail_of(valid, own, other, query, hidden, gain, weight):
    tokens, features = query.shape
    half = jax.ShapeDtypeStruct((tokens // 2, features), jnp.bfloat16)
    return pl.pallas_call(
        tail_kernel,
        out_shape=(half, half),
        in_specs=[smem()] + [vmem()] * 6,
        out_specs=(vmem(), vmem()),
        scratch_shapes=[pltpu.VMEM(half.shape, jnp.bfloat16)],
        compiler_params=limit(24),
        cost_estimate=cost(3),
        name="tail_of",
    )(valid, own, other, query, hidden, gain, weight)


def head_kernel(
    valid_ref, own_ref, other_ref, query_ref, hidden_ref, gain_ref, weight,
    tail_residual, tail_normed, taps_ref, out_ref, residual, partial_ref, attended, normed_ref
):
    count, features = residual.shape
    step = count // 2
    project(
        valid_ref, own_ref, other_ref, query_ref.at[:count, :], hidden_ref.at[:count, :],
        gain_ref, weight, 0, attended, residual, normed_ref,
    )
    for s in range(0, features, LANES):
        w = min(LANES, features - s)
        taps = [taps_ref[j : j + 1, s : s + w] for j in range(3)]
        frames = [
            ref[t * step : (t + 1) * step, s : s + w].astype(jnp.float32)
            for ref in (normed_ref, tail_normed)
            for t in range(2)
        ]
        partial_ref[:step, s : s + w] = taps[0] * frames[0]
        partial_ref[step:, s : s + w] = taps[0] * frames[1] + taps[1] * frames[0]
        for t in range(2):
            total = taps[0] * frames[t + 2] + taps[1] * frames[t + 1] + taps[2] * frames[t]
            temporal = total.astype(jnp.bfloat16).astype(jnp.float32)
            at = slice(t * step, (t + 1) * step)
            here = tail_residual[at, s : s + w].astype(jnp.float32)
            out_ref[at, s : s + w] = (here + temporal).astype(jnp.bfloat16)


def head_of(valid, own, other, query, hidden, gain, weight, tail_residual, tail_normed, taps):
    tokens, features = query.shape
    half = (tokens // 2, features)
    return pl.pallas_call(
        head_kernel,
        grid=(1,),
        out_shape=(
            jax.ShapeDtypeStruct(query.shape, jnp.bfloat16),
            jax.ShapeDtypeStruct(half, jnp.bfloat16),
            jax.ShapeDtypeStruct(half, jnp.float32),
        ),
        in_specs=[smem()] + [vmem()] * 9,
        out_specs=(pl.BlockSpec(half, lambda i: (1, 0)), vmem(), vmem()),
        scratch_shapes=[pltpu.VMEM(half, jnp.bfloat16), pltpu.VMEM(half, jnp.bfloat16)],
        compiler_params=limit(24),
        cost_estimate=cost(3),
        name="head_of",
    )(valid, own, other, query, hidden, gain, weight, tail_residual, tail_normed, taps)


def finish_kernel(unused_ref, residual_ref, partial_ref, halo_ref, taps_ref, out_ref):
    count, features = residual_ref.shape
    step = count // 2
    for s in range(0, features, LANES):
        w = min(LANES, features - s)
        taps = [taps_ref[j : j + 1, s : s + w] for j in range(3)]
        oldest = halo_ref[:step, s : s + w].astype(jnp.float32)
        older = halo_ref[step:, s : s + w].astype(jnp.float32)
        totals = [
            partial_ref[:step, s : s + w] + taps[1] * older + taps[2] * oldest,
            partial_ref[step:, s : s + w] + taps[2] * older,
        ]
        for t, total in enumerate(totals):
            temporal = total.astype(jnp.bfloat16).astype(jnp.float32)
            at = slice(t * step, (t + 1) * step)
            here = residual_ref[at, s : s + w].astype(jnp.float32)
            out_ref[at, s : s + w] = (here + temporal).astype(jnp.bfloat16)


def finish(out, residual, partial, halo, taps):
    return pl.pallas_call(
        finish_kernel,
        grid=(1,),
        out_shape=jax.ShapeDtypeStruct(out.shape, out.dtype),
        in_specs=[pl.BlockSpec(memory_space=pl.ANY)] + [vmem()] * 4,
        out_specs=pl.BlockSpec(residual.shape, lambda i: (0, 0)),
        input_output_aliases={0: 0},
        compiler_params=limit(8),
        cost_estimate=cost(1),
        name="finish",
    )(out, residual, partial, halo, taps)


def body(query_in, key_in, value_in, hidden_in, out_weight, norm_gain, temporal_taps, block_valid):
    frames, rows_dev, width_cols, features = query_in.shape
    tokens = frames * rows_dev * width_cols
    query = query_in.reshape(tokens, features)
    hidden = hidden_in.reshape(tokens, features)
    swap = [(0, 1), (1, 0)]
    value = value_in.reshape(tokens, features)
    turned = turn(live_of(block_valid, tokens), key_in.reshape(tokens, features))
    send = local_states(turned, value, False)
    fetched = lax.ppermute(send, "core", swap)
    keep = local_states(turned, value, True)
    mine = (keep + fetched.astype(jnp.float32)).astype(jnp.bfloat16)
    piece = ROWS // (Z * Y)
    got = lax.all_to_all(mine, ("z", "y"), 0, 0, tiled=True).reshape(Z * Y, piece, LANES)
    prefix, whole = prefixes(got)
    wholes = lax.all_to_all(whole, "x", 0, 0, tiled=True)
    own = lax.all_to_all(totals(prefix, wholes), ("z", "y"), 0, 0, tiled=True)
    own = own.reshape(ROWS, LANES)
    other = lax.ppermute(own, "core", swap)
    gain = norm_gain.reshape(1, features)
    shared = (block_valid, own, other, query, hidden, gain, out_weight)
    tail_residual, tail_normed = tail_of(*shared)
    halo = lax.ppermute(tail_normed, ("x", "z"), [(i, i + 1) for i in range(X * Z - 1)])
    out, residual, partial = head_of(*shared, tail_residual, tail_normed, temporal_taps)
    mixed = finish(out, residual, partial, halo, temporal_taps)
    return mixed.reshape(query_in.shape)


def solution(mesh):
    fine = Mesh(mesh.devices.reshape(X, Z, Y, C), ("x", "z", "y", "core"))
    token = P(("x", "z"), ("y", "core"), None, None)
    placed = (token, token, token, token, P(), P(), P(), P(("x", "z")))

    return jax.shard_map(body, mesh=fine, in_specs=placed, out_specs=token, check_vma=False)
```

```python
import functools

import jax
import jax.numpy as jnp
from jax import lax
from jax.experimental import pallas as pl
from jax.experimental.pallas import tpu as pltpu
from jax.sharding import Mesh, PartitionSpec as P


HEADS = 20
DH = 112
LANES = 128
PIECE = 14
GROUP = HEADS // 2
ROWS = 1024
EPS_DEN = 1e-06
EPS_NORM = 1e-06
X, Z, Y, C = 4, 8, 4, 2
CHUNK = 512
SPLIT = 1152


def smem():
    return pl.BlockSpec(memory_space=pltpu.SMEM)


def vmem():
    return pl.BlockSpec(memory_space=pltpu.VMEM)


def limit(mib):
    return pltpu.CompilerParams(vmem_limit_bytes=mib << 20)


def cost(micros):
    return pl.CostEstimate(flops=micros * 1_000_000_000, bytes_accessed=1 << 20, transcendentals=0)


def lane_of(shape):
    return lax.broadcasted_iota(jnp.int32, shape, 1)


def place_of(h):
    return (h * DH) // LANES, (h * DH) % LANES


def free_of(h):
    return ((h + 1) * DH) % LANES


def group_states(group, turned, value_ref, out_ref):
    tokens, features = value_ref.shape
    lane = lane_of((tokens, LANES))
    one = jnp.ones((tokens, LANES), jnp.bfloat16)
    lanes = lane_of((DH, LANES))

    def values_at(start):
        width = min(LANES, features - start)
        values = value_ref[:, start : start + width]
        if width < LANES:
            values = jnp.concatenate(
                [values, jnp.zeros((tokens, LANES - width), jnp.bfloat16)], axis=1
            )
        return values

    def head(h):
        tile, off = place_of(h)
        keys = turned[h * DH : (h + 1) * DH, :]
        low = values_at(tile * LANES)
        if off == 0:
            low = jnp.where(lane == DH, one, low)
            return jnp.dot(keys, low, preferred_element_type=jnp.float32)
        high = jnp.where(lane == free_of(h), one, values_at((tile + 1) * LANES))
        wide = jnp.dot(
            keys, jnp.concatenate([low, high], axis=1), preferred_element_type=jnp.float32
        )
        return jnp.where(lanes >= off, wide[:, :LANES], wide[:, LANES:])

    end = group * GROUP + GROUP - 1
    last = head(end)
    for p in range(GROUP - 1):
        h = group * GROUP + p
        free = free_of(h)
        state = head(h)
        if p < 8:
            shift = (free + 2 - place_of(end)[1] - PIECE * p) % LANES
            mask = (lanes >= free + 2) & (lanes < free + 16)
        else:
            shift = (free + 1 - free_of(end)) % LANES
            mask = lanes == free + 1
        moved = pltpu.roll(last, shift, axis=1) if shift else last
        state = jnp.where(mask, moved, state)
        out_ref[p * DH : (p + 1) * DH, :] = state.astype(out_ref.dtype)
    rest = ROWS - (GROUP - 1) * DH
    out_ref[(GROUP - 1) * DH :, :] = jnp.zeros((rest, LANES), out_ref.dtype)


def live_kernel(valid_ref, out_ref):
    tokens = out_ref.shape[0]
    row = lax.broadcasted_iota(jnp.int32, out_ref.shape, 0)
    live = row < valid_ref[0] * (tokens // 4)
    out_ref[...] = jnp.where(live, 1.0, 0.0).astype(jnp.bfloat16)


def live_of(valid, tokens):
    return pl.pallas_call(
        live_kernel,
        out_shape=jax.ShapeDtypeStruct((tokens, LANES), jnp.bfloat16),
        in_specs=[smem()],
        out_specs=vmem(),
        compiler_params=limit(2),
        cost_estimate=cost(8),
        name="live_of",
    )(valid)


def turn_kernel(live_ref, key_ref, out_ref):
    _, features = key_ref.shape
    live = live_ref[...]
    for start in range(0, features, LANES):
        width = min(LANES, features - start)
        keys = jnp.maximum(key_ref[:, start : start + width], 0) * live[:, :width]
        out_ref[start : start + width, :] = keys.T


def turn(live, key):
    tokens, features = key.shape
    return pl.pallas_call(
        turn_kernel,
        out_shape=jax.ShapeDtypeStruct((features, tokens), jnp.bfloat16),
        in_specs=[vmem(), vmem()],
        out_specs=vmem(),
        compiler_params=limit(8),
        name="turn",
    )(live, key)


def state_kernel(mine, turned, value_ref, out_ref):
    core = lax.axis_index("core")
    for group in range(2):

        @pl.when(core == (group if mine else 1 - group))
        def _():
            group_states(group, turned, value_ref, out_ref)


def local_states(turned, value, mine):
    return pl.pallas_call(
        functools.partial(state_kernel, mine),
        out_shape=jax.ShapeDtypeStruct((ROWS, LANES), jnp.float32 if mine else jnp.bfloat16),
        in_specs=[vmem(), vmem()],
        out_specs=vmem(),
        compiler_params=limit(8),
        cost_estimate=cost(1),
        name="kept_states" if mine else "sent_states",
    )(turned, value)


def prefix_kernel(got_ref, prefix_ref, whole_ref):
    total = jnp.zeros(prefix_ref.shape[1:], jnp.float32)
    for z in range(Z):
        for y in range(Y):
            total = total + got_ref[z * Y + y].astype(jnp.float32)
        prefix_ref[z] = total
    for x in range(X):
        whole_ref[x] = total


def prefixes(got):
    piece = got.shape[1:]
    return pl.pallas_call(
        prefix_kernel,
        out_shape=(
            jax.ShapeDtypeStruct((Z,) + piece, jnp.float32),
            jax.ShapeDtypeStruct((X,) + piece, jnp.float32),
        ),
        in_specs=[vmem()],
        out_specs=(vmem(), vmem()),
        compiler_params=limit(4),
        cost_estimate=cost(8),
        name="prefixes",
    )(got)


def totals_kernel(prefix_ref, whole_ref, out_ref):
    place = lax.axis_index("x")
    before = jnp.zeros(prefix_ref.shape[1:], jnp.float32)
    for x in range(X):
        before = before + jnp.where(x < place, whole_ref[x], 0.0)
    for z in range(Z):
        total = (prefix_ref[z] + before).astype(jnp.bfloat16)
        for y in range(Y):
            out_ref[z * Y + y] = total


def totals(prefix, whole):
    piece = prefix.shape[1:]
    return pl.pallas_call(
        totals_kernel,
        out_shape=jax.ShapeDtypeStruct((Z * Y,) + piece, jnp.bfloat16),
        in_specs=[vmem(), vmem()],
        out_specs=vmem(),
        compiler_params=limit(4),
        cost_estimate=cost(8),
        name="totals",
    )(prefix, whole)


def attend_rows(valid_ref, own_ref, other_ref, query_ref, first, attended):
    count, features = query_ref.shape
    step = count // 2
    own = lax.axis_index("core")
    lanes = lane_of((DH, LANES))
    zero = jnp.zeros((DH, LANES), jnp.bfloat16)

    def stored(group, p):
        at = slice(p * DH, (p + 1) * DH)
        return jnp.where(own == group, own_ref[at, :], other_ref[at, :])

    def unpack(group):
        packed = [stored(group, p) for p in range(GROUP - 1)]
        end = group * GROUP + GROUP - 1
        off = place_of(end)[1]
        last = jnp.zeros((DH, LANES), jnp.float32)
        for p in range(GROUP - 1):
            free = free_of(group * GROUP + p)
            if p < 8:
                shift = (off + PIECE * p - free - 2) % LANES
                start = (off + PIECE * p) % LANES
                mask = (lanes >= start) & (lanes < start + PIECE)
                if start + PIECE > LANES:
                    mask = mask | (lanes < start + PIECE - LANES)
            else:
                shift = (free_of(end) - free - 1) % LANES
                mask = lanes == free_of(end)
            wide = packed[p].astype(jnp.float32)
            moved = pltpu.roll(wide, shift, axis=1) if shift else wide
            last = jnp.where(mask, moved, last)
        return packed + [last.astype(jnp.bfloat16)]

    def window(h, packed):
        off = place_of(h)[1]
        if off == 0:
            return jnp.where(lanes <= DH, packed, zero)
        low = jnp.where(lanes >= off, packed, zero)
        high = jnp.where(lanes <= off - 16, packed, zero)
        return jnp.concatenate([low, high], axis=1)

    row = lax.broadcasted_iota(jnp.int32, (count, 1), 0)
    live = (row + first * step < valid_ref[0] * step).astype(jnp.float32)
    lane = lane_of((count, LANES))
    carry = None
    for group in range(2):
        unpacked = unpack(group)
        for p in range(GROUP):
            h = group * GROUP + p
            tile, off = place_of(h)
            start = tile * LANES
            stop = min(start + (LANES if off == 0 else 2 * LANES), features)
            wide = window(h, unpacked[p])
            parts = [wide]
            if off:
                parts.insert(0, jnp.zeros((off, wide.shape[1]), jnp.bfloat16))
            rest = stop - start - off - DH
            if rest:
                parts.append(jnp.zeros((rest, wide.shape[1]), jnp.bfloat16))
            matrix = jnp.concatenate(parts, axis=0) if len(parts) > 1 else wide
            query = jnp.maximum(query_ref[:, start:stop], 0)
            got = jnp.dot(query, matrix, preferred_element_type=jnp.float32)
            below = got[:, off + DH : off + DH + 1] + EPS_DEN
            scale = jnp.broadcast_to(live / below, (count, LANES))
            low = got[:, :LANES] * scale
            if off == 0:
                carry = low
                continue
            full = jnp.where(lane >= off, low, carry)
            attended[:, start : start + LANES] = full.astype(jnp.bfloat16)
            carry = got[:, LANES:] * scale
    left = features % LANES
    if left:
        attended[:, features - left :] = carry[:, :left].astype(jnp.bfloat16)


def project_columns(attended, hidden_ref, weight, residual, start, stop):
    for s in range(start, stop, CHUNK):
        at = slice(s, min(s + CHUNK, stop))
        projected = jnp.dot(attended[...], weight[:, at], preferred_element_type=jnp.float32)
        rounded = (hidden_ref[:, at].astype(jnp.float32) + projected).astype(jnp.bfloat16)
        residual[:, at.start - start : at.stop - start] = rounded


def inverse_of(parts):
    count = parts[0].shape[0]
    features = sum(part.shape[1] for part in parts)
    squares = jnp.zeros((count, LANES), jnp.float32)
    for part in parts:
        width = part.shape[1]
        for s in range(0, width, LANES):
            w = min(LANES, width - s)
            wide = part[:, s : s + w].astype(jnp.float32)
            wide = wide * wide
            if w < LANES:
                wide = jnp.concatenate([wide, jnp.zeros((count, LANES - w), jnp.float32)], axis=1)
            squares = squares + wide
    mean = jnp.sum(squares, axis=1, keepdims=True) / features
    return jnp.broadcast_to(lax.rsqrt(mean + EPS_NORM), (count, LANES))


def normed_at(parts, inverse, gain_ref, s, w):
    here = at_columns(parts, s, w)
    normed = (here * inverse[:, :w] * gain_ref[:, s : s + w]).astype(jnp.bfloat16)
    return normed.astype(jnp.float32)


def at_columns(parts, s, w):
    for part in parts:
        if s < part.shape[1]:
            return part[:, s : s + w].astype(jnp.float32)
        s -= part.shape[1]


def tail_a_kernel(
    valid_ref, own_ref, other_ref, query_ref, hidden_ref, weight, attended, residual
):
    half = query_ref.shape[0] // 2
    attend_rows(valid_ref, own_ref, other_ref, query_ref.at[half:, :], 2, attended)
    project_columns(attended, hidden_ref.at[half:, :], weight, residual, 0, SPLIT)


def tail_a(valid, own, other, query, hidden, weight):
    tokens, features = query.shape
    return pl.pallas_call(
        tail_a_kernel,
        out_shape=(
            jax.ShapeDtypeStruct((tokens // 2, features), jnp.bfloat16),
            jax.ShapeDtypeStruct((tokens // 2, SPLIT), jnp.bfloat16),
        ),
        in_specs=[smem()] + [vmem()] * 5,
        out_specs=(vmem(), vmem()),
        compiler_params=limit(24),
        cost_estimate=cost(3),
        name="tail_a",
    )(valid, own, other, query, hidden, weight)


def tail_b_kernel(attended, hidden_ref, weight, residual):
    half, features = attended.shape
    project_columns(attended, hidden_ref.at[half:, :], weight, residual, SPLIT, features)


def tail_b(attended, hidden, weight):
    half, features = attended.shape
    return pl.pallas_call(
        tail_b_kernel,
        out_shape=jax.ShapeDtypeStruct((half, features - SPLIT), jnp.bfloat16),
        in_specs=[vmem()] * 3,
        out_specs=vmem(),
        compiler_params=limit(24),
        cost_estimate=cost(1),
        name="tail_b",
    )(attended, hidden, weight)


def head_kernel(
    valid_ref,
    own_ref,
    other_ref,
    query_ref,
    hidden_ref,
    weight,
    gain_ref,
    left_ref,
    right_ref,
    taps_ref,
    out_ref,
    residual,
    partial_ref,
    attended,
):
    count, features = residual.shape
    step = count // 2
    attend_rows(valid_ref, own_ref, other_ref, query_ref.at[:count, :], 0, attended)
    project_columns(attended, hidden_ref.at[:count, :], weight, residual, 0, features)
    head, tail = (residual,), (left_ref, right_ref)
    head_inverse, tail_inverse = inverse_of(head), inverse_of(tail)
    for s in range(0, features, LANES):
        w = min(LANES, features - s)
        taps = [taps_ref[j : j + 1, s : s + w] for j in range(3)]
        early = normed_at(head, head_inverse, gain_ref, s, w)
        late = normed_at(tail, tail_inverse, gain_ref, s, w)
        frames = [early[:step], early[step:], late[:step], late[step:]]
        partial_ref[:step, s : s + w] = taps[0] * frames[0]
        partial_ref[step:, s : s + w] = taps[0] * frames[1] + taps[1] * frames[0]
        here = at_columns(tail, s, w)
        for t in range(2):
            total = taps[0] * frames[t + 2] + taps[1] * frames[t + 1] + taps[2] * frames[t]
            temporal = total.astype(jnp.bfloat16).astype(jnp.float32)
            at = slice(t * step, (t + 1) * step)
            out_ref[at, s : s + w] = (here[at] + temporal).astype(jnp.bfloat16)


def head_of(valid, own, other, query, hidden, weight, gain, left, right, taps):
    tokens, features = query.shape
    half = (tokens // 2, features)
    return pl.pallas_call(
        head_kernel,
        grid=(1,),
        out_shape=(
            jax.ShapeDtypeStruct(query.shape, jnp.bfloat16),
            jax.ShapeDtypeStruct(half, jnp.bfloat16),
            jax.ShapeDtypeStruct(half, jnp.float32),
        ),
        in_specs=[smem()] + [vmem()] * 9,
        out_specs=(pl.BlockSpec(half, lambda i: (1, 0)), vmem(), vmem()),
        scratch_shapes=[pltpu.VMEM(half, jnp.bfloat16)],
        compiler_params=limit(24),
        cost_estimate=cost(3),
        name="head_of",
    )(valid, own, other, query, hidden, weight, gain, left, right, taps)


def finish_kernel(
    unused_ref, residual_ref, partial_ref, left_ref, right_ref, gain_ref, taps_ref, out_ref
):
    count, features = residual_ref.shape
    step = count // 2
    halo = (left_ref, right_ref)
    inverse = inverse_of(halo)
    for s in range(0, features, LANES):
        w = min(LANES, features - s)
        taps = [taps_ref[j : j + 1, s : s + w] for j in range(3)]
        before = normed_at(halo, inverse, gain_ref, s, w)
        oldest, older = before[:step], before[step:]
        totals = [
            partial_ref[:step, s : s + w] + taps[1] * older + taps[2] * oldest,
            partial_ref[step:, s : s + w] + taps[2] * older,
        ]
        for t, total in enumerate(totals):
            temporal = total.astype(jnp.bfloat16).astype(jnp.float32)
            at = slice(t * step, (t + 1) * step)
            here = residual_ref[at, s : s + w].astype(jnp.float32)
            out_ref[at, s : s + w] = (here + temporal).astype(jnp.bfloat16)


def finish(out, residual, partial, left, right, gain, taps):
    return pl.pallas_call(
        finish_kernel,
        grid=(1,),
        out_shape=jax.ShapeDtypeStruct(out.shape, out.dtype),
        in_specs=[pl.BlockSpec(memory_space=pl.ANY)] + [vmem()] * 6,
        out_specs=pl.BlockSpec(residual.shape, lambda i: (0, 0)),
        input_output_aliases={0: 0},
        compiler_params=limit(8),
        cost_estimate=cost(1),
        name="finish",
    )(out, residual, partial, left, right, gain, taps)


def body(query_in, key_in, value_in, hidden_in, out_weight, norm_gain, temporal_taps, block_valid):
    frames, rows_dev, width_cols, features = query_in.shape
    tokens = frames * rows_dev * width_cols
    query = query_in.reshape(tokens, features)
    hidden = hidden_in.reshape(tokens, features)
    swap = [(0, 1), (1, 0)]
    value = value_in.reshape(tokens, features)
    turned = turn(live_of(block_valid, tokens), key_in.reshape(tokens, features))
    send = local_states(turned, value, False)
    fetched = lax.ppermute(send, "core", swap)
    keep = local_states(turned, value, True)
    mine = (keep + fetched.astype(jnp.float32)).astype(jnp.bfloat16)
    piece = ROWS // (Z * Y)
    got = lax.all_to_all(mine, ("z", "y"), 0, 0, tiled=True).reshape(Z * Y, piece, LANES)
    prefix, whole = prefixes(got)
    wholes = lax.all_to_all(whole, "x", 0, 0, tiled=True)
    own = lax.all_to_all(totals(prefix, wholes), ("z", "y"), 0, 0, tiled=True)
    own = own.reshape(ROWS, LANES)
    other = lax.ppermute(own, "core", swap)
    gain = norm_gain.reshape(1, features)
    shared = (block_valid, own, other, query, hidden, out_weight)
    chain = [(i, i + 1) for i in range(X * Z - 1)]
    attended, left = tail_a(*shared)
    halo_left = lax.ppermute(left, ("x", "z"), chain)
    right = tail_b(attended, hidden, out_weight)
    halo_right = lax.ppermute(right, ("x", "z"), chain)
    out, residual, partial = head_of(*shared, gain, left, right, temporal_taps)
    mixed = finish(out, residual, partial, halo_left, halo_right, gain, temporal_taps)
    return mixed.reshape(query_in.shape)


def solution(mesh):
    fine = Mesh(mesh.devices.reshape(X, Z, Y, C), ("x", "z", "y", "core"))
    token = P(("x", "z"), ("y", "core"), None, None)
    placed = (token, token, token, token, P(), P(), P(), P(("x", "z")))

    return jax.shard_map(body, mesh=fine, in_specs=placed, out_specs=token, check_vma=False)
```

```python
import functools

import jax
import jax.numpy as jnp
from jax import lax
from jax.experimental import pallas as pl
from jax.experimental.pallas import tpu as pltpu
from jax.sharding import Mesh, PartitionSpec as P


HEADS = 20
DH = 112
LANES = 128
PIECE = 14
GROUP = HEADS // 2
ROWS = 1024
EPS_DEN = 1e-06
EPS_NORM = 1e-06
X, Z, Y, C = 4, 8, 4, 2
CHUNK = 512
SPLIT = 1408


def smem():
    return pl.BlockSpec(memory_space=pltpu.SMEM)


def vmem():
    return pl.BlockSpec(memory_space=pltpu.VMEM)


def limit(mib):
    return pltpu.CompilerParams(vmem_limit_bytes=mib << 20)


def cost(micros):
    return pl.CostEstimate(flops=micros * 1_000_000_000, bytes_accessed=1 << 20, transcendentals=0)


def lane_of(shape):
    return lax.broadcasted_iota(jnp.int32, shape, 1)


def place_of(h):
    return (h * DH) // LANES, (h * DH) % LANES


def free_of(h):
    return ((h + 1) * DH) % LANES


def group_states(group, turned, value_ref, out_ref):
    tokens, features = value_ref.shape
    lane = lane_of((tokens, LANES))
    one = jnp.ones((tokens, LANES), jnp.bfloat16)
    lanes = lane_of((DH, LANES))

    def values_at(start):
        width = min(LANES, features - start)
        values = value_ref[:, start : start + width]
        if width < LANES:
            values = jnp.concatenate(
                [values, jnp.zeros((tokens, LANES - width), jnp.bfloat16)], axis=1
            )
        return values

    def head(h):
        tile, off = place_of(h)
        keys = turned[h * DH : (h + 1) * DH, :]
        low = values_at(tile * LANES)
        if off == 0:
            low = jnp.where(lane == DH, one, low)
            return jnp.dot(keys, low, preferred_element_type=jnp.float32)
        high = jnp.where(lane == free_of(h), one, values_at((tile + 1) * LANES))
        wide = jnp.dot(
            keys, jnp.concatenate([low, high], axis=1), preferred_element_type=jnp.float32
        )
        return jnp.where(lanes >= off, wide[:, :LANES], wide[:, LANES:])

    end = group * GROUP + GROUP - 1
    last = head(end)
    for p in range(GROUP - 1):
        h = group * GROUP + p
        free = free_of(h)
        state = head(h)
        if p < 8:
            shift = (free + 2 - place_of(end)[1] - PIECE * p) % LANES
            mask = (lanes >= free + 2) & (lanes < free + 16)
        else:
            shift = (free + 1 - free_of(end)) % LANES
            mask = lanes == free + 1
        moved = pltpu.roll(last, shift, axis=1) if shift else last
        state = jnp.where(mask, moved, state)
        out_ref[p * DH : (p + 1) * DH, :] = state.astype(out_ref.dtype)
    rest = ROWS - (GROUP - 1) * DH
    out_ref[(GROUP - 1) * DH :, :] = jnp.zeros((rest, LANES), out_ref.dtype)


def live_kernel(valid_ref, out_ref):
    tokens = out_ref.shape[0]
    row = lax.broadcasted_iota(jnp.int32, out_ref.shape, 0)
    live = row < valid_ref[0] * (tokens // 4)
    out_ref[...] = jnp.where(live, 1.0, 0.0).astype(jnp.bfloat16)


def live_of(valid, tokens):
    return pl.pallas_call(
        live_kernel,
        out_shape=jax.ShapeDtypeStruct((tokens, LANES), jnp.bfloat16),
        in_specs=[smem()],
        out_specs=vmem(),
        compiler_params=limit(2),
        cost_estimate=cost(8),
        name="live_of",
    )(valid)


def turn_kernel(live_ref, key_ref, out_ref):
    _, features = key_ref.shape
    live = live_ref[...]
    for start in range(0, features, LANES):
        width = min(LANES, features - start)
        keys = jnp.maximum(key_ref[:, start : start + width], 0) * live[:, :width]
        out_ref[start : start + width, :] = keys.T


def turn(live, key):
    tokens, features = key.shape
    return pl.pallas_call(
        turn_kernel,
        out_shape=jax.ShapeDtypeStruct((features, tokens), jnp.bfloat16),
        in_specs=[vmem(), vmem()],
        out_specs=vmem(),
        compiler_params=limit(8),
        name="turn",
    )(live, key)


def state_kernel(mine, turned, value_ref, out_ref):
    core = lax.axis_index("core")
    for group in range(2):

        @pl.when(core == (group if mine else 1 - group))
        def _():
            group_states(group, turned, value_ref, out_ref)


def local_states(turned, value, mine):
    return pl.pallas_call(
        functools.partial(state_kernel, mine),
        out_shape=jax.ShapeDtypeStruct((ROWS, LANES), jnp.float32 if mine else jnp.bfloat16),
        in_specs=[vmem(), vmem()],
        out_specs=vmem(),
        compiler_params=limit(8),
        cost_estimate=cost(1),
        name="kept_states" if mine else "sent_states",
    )(turned, value)


def prefix_kernel(got_ref, prefix_ref, whole_ref):
    total = jnp.zeros(prefix_ref.shape[1:], jnp.float32)
    for z in range(Z):
        for y in range(Y):
            total = total + got_ref[z * Y + y].astype(jnp.float32)
        prefix_ref[z] = total
    for x in range(X):
        whole_ref[x] = total


def prefixes(got):
    piece = got.shape[1:]
    return pl.pallas_call(
        prefix_kernel,
        out_shape=(
            jax.ShapeDtypeStruct((Z,) + piece, jnp.float32),
            jax.ShapeDtypeStruct((X,) + piece, jnp.float32),
        ),
        in_specs=[vmem()],
        out_specs=(vmem(), vmem()),
        compiler_params=limit(4),
        cost_estimate=cost(8),
        name="prefixes",
    )(got)


def totals_kernel(prefix_ref, whole_ref, out_ref):
    place = lax.axis_index("x")
    before = jnp.zeros(prefix_ref.shape[1:], jnp.float32)
    for x in range(X):
        before = before + jnp.where(x < place, whole_ref[x], 0.0)
    for z in range(Z):
        total = (prefix_ref[z] + before).astype(jnp.bfloat16)
        for y in range(Y):
            out_ref[z * Y + y] = total


def totals(prefix, whole):
    piece = prefix.shape[1:]
    return pl.pallas_call(
        totals_kernel,
        out_shape=jax.ShapeDtypeStruct((Z * Y,) + piece, jnp.bfloat16),
        in_specs=[vmem(), vmem()],
        out_specs=vmem(),
        compiler_params=limit(4),
        cost_estimate=cost(8),
        name="totals",
    )(prefix, whole)


def unpack(group, stored):
    lanes = lane_of((DH, LANES))
    packed = [stored(group, p) for p in range(GROUP - 1)]
    end = group * GROUP + GROUP - 1
    off = place_of(end)[1]
    last = jnp.zeros((DH, LANES), jnp.float32)
    for p in range(GROUP - 1):
        free = free_of(group * GROUP + p)
        if p < 8:
            shift = (off + PIECE * p - free - 2) % LANES
            start = (off + PIECE * p) % LANES
            mask = (lanes >= start) & (lanes < start + PIECE)
            if start + PIECE > LANES:
                mask = mask | (lanes < start + PIECE - LANES)
        else:
            shift = (free_of(end) - free - 1) % LANES
            mask = lanes == free_of(end)
        wide = packed[p].astype(jnp.float32)
        moved = pltpu.roll(wide, shift, axis=1) if shift else wide
        last = jnp.where(mask, moved, last)
    return packed + [last.astype(jnp.bfloat16)]


def window(h, packed):
    lanes = lane_of((DH, LANES))
    zero = jnp.zeros((DH, LANES), jnp.bfloat16)
    off = place_of(h)[1]
    if off == 0:
        return jnp.where(lanes <= DH, packed, zero)
    low = jnp.where(lanes >= off, packed, zero)
    high = jnp.where(lanes <= off - 16, packed, zero)
    return jnp.concatenate([low, high], axis=1)


def attend_group(group, stored, query_ref, live, attended, carry):
    count, features = query_ref.shape
    lane = lane_of((count, LANES))
    unpacked = unpack(group, stored)
    for p in range(GROUP):
        h = group * GROUP + p
        tile, off = place_of(h)
        start = tile * LANES
        stop = min(start + (LANES if off == 0 else 2 * LANES), features)
        wide = window(h, unpacked[p])
        parts = [wide]
        if off:
            parts.insert(0, jnp.zeros((off, wide.shape[1]), jnp.bfloat16))
        rest = stop - start - off - DH
        if rest:
            parts.append(jnp.zeros((rest, wide.shape[1]), jnp.bfloat16))
        matrix = jnp.concatenate(parts, axis=0) if len(parts) > 1 else wide
        query = jnp.maximum(query_ref[:, start:stop], 0)
        got = jnp.dot(query, matrix, preferred_element_type=jnp.float32)
        below = got[:, off + DH : off + DH + 1] + EPS_DEN
        scale = jnp.broadcast_to(live / below, (count, LANES))
        low = got[:, :LANES] * scale
        if off == 0:
            carry = low
            continue
        full = jnp.where(lane >= off, low, carry)
        attended[:, start : start + LANES] = full.astype(jnp.bfloat16)
        carry = got[:, LANES:] * scale
    return carry


def live_rows(valid_ref, count, first):
    step = count // 2
    row = lax.broadcasted_iota(jnp.int32, (count, 1), 0)
    return (row + first * step < valid_ref[0] * step).astype(jnp.float32)


def store_end(attended, carry):
    left = attended.shape[1] % LANES
    if left:
        attended[:, attended.shape[1] - left :] = carry[:, :left].astype(jnp.bfloat16)


def attend_rows(valid_ref, own_ref, other_ref, query_ref, first, attended):
    own = lax.axis_index("core")

    def stored(group, p):
        at = slice(p * DH, (p + 1) * DH)
        return jnp.where(own == group, own_ref[at, :], other_ref[at, :])

    live = live_rows(valid_ref, query_ref.shape[0], first)
    carry = None
    for group in range(2):
        carry = attend_group(group, stored, query_ref, live, attended, carry)
    store_end(attended, carry)


def attend_half(group, valid_ref, state_ref, query_ref, attended):
    count = query_ref.shape[0]

    def stored(group, p):
        return state_ref[p * DH : (p + 1) * DH, :]

    live = live_rows(valid_ref, count, 2)
    carry = jnp.zeros((count, LANES), jnp.float32)
    carry = attend_group(group, stored, query_ref, live, attended, carry)
    if group:
        store_end(attended, carry)
    else:
        tile = place_of(GROUP)[0] * LANES
        attended[:, tile : tile + LANES] = carry.astype(jnp.bfloat16)


def tail_own_kernel(valid_ref, own_ref, query_ref, attended):
    half = query_ref.shape[0] // 2
    core = lax.axis_index("core")
    for group in range(2):

        @pl.when(core == group)
        def _():
            attend_half(group, valid_ref, own_ref, query_ref.at[half:, :], attended)


def tail_own(valid, own, query):
    tokens, features = query.shape
    return pl.pallas_call(
        tail_own_kernel,
        out_shape=jax.ShapeDtypeStruct((tokens // 2, features), jnp.bfloat16),
        in_specs=[smem(), vmem(), vmem()],
        out_specs=vmem(),
        compiler_params=limit(8),
        cost_estimate=cost(1),
        name="tail_own",
    )(valid, own, query)


def project_columns(attended, hidden_ref, weight, residual, start, stop):
    for s in range(start, stop, CHUNK):
        at = slice(s, min(s + CHUNK, stop))
        projected = jnp.dot(attended[...], weight[:, at], preferred_element_type=jnp.float32)
        rounded = (hidden_ref[:, at].astype(jnp.float32) + projected).astype(jnp.bfloat16)
        residual[:, at.start - start : at.stop - start] = rounded


def inverse_of(parts):
    count = parts[0].shape[0]
    features = sum(part.shape[1] for part in parts)
    squares = jnp.zeros((count, LANES), jnp.float32)
    for part in parts:
        width = part.shape[1]
        for s in range(0, width, LANES):
            w = min(LANES, width - s)
            wide = part[:, s : s + w].astype(jnp.float32)
            wide = wide * wide
            if w < LANES:
                wide = jnp.concatenate([wide, jnp.zeros((count, LANES - w), jnp.float32)], axis=1)
            squares = squares + wide
    mean = jnp.sum(squares, axis=1, keepdims=True) / features
    return jnp.broadcast_to(lax.rsqrt(mean + EPS_NORM), (count, LANES))


def normed_at(parts, inverse, gain_ref, s, w):
    here = at_columns(parts, s, w)
    normed = (here * inverse[:, :w] * gain_ref[:, s : s + w]).astype(jnp.bfloat16)
    return normed.astype(jnp.float32)


def at_columns(parts, s, w):
    for part in parts:
        if s < part.shape[1]:
            return part[:, s : s + w].astype(jnp.float32)
        s -= part.shape[1]


def tail_a_kernel(
    valid_ref, other_ref, query_ref, hidden_ref, weight, own_attended, attended, residual
):
    count, features = attended.shape
    core = lax.axis_index("core")
    tile, off = place_of(GROUP)
    shared = slice(tile * LANES, (tile + 1) * LANES)
    lane = lane_of((count, LANES))
    for group in range(2):

        @pl.when(core == 1 - group)
        def _():
            attend_half(group, valid_ref, other_ref, query_ref.at[count:, :], attended)
            done = slice(shared.stop, features) if group == 0 else slice(0, shared.start)
            attended[:, done] = own_attended[:, done]
            first = (attended if group == 0 else own_attended)[:, shared]
            second = (own_attended if group == 0 else attended)[:, shared]
            attended[:, shared] = jnp.where(lane < off, first, second)

    project_columns(attended, hidden_ref.at[count:, :], weight, residual, 0, SPLIT)


def tail_a(valid, other, query, hidden, weight, own_attended):
    tokens, features = query.shape
    return pl.pallas_call(
        tail_a_kernel,
        out_shape=(
            jax.ShapeDtypeStruct((tokens // 2, features), jnp.bfloat16),
            jax.ShapeDtypeStruct((tokens // 2, SPLIT), jnp.bfloat16),
        ),
        in_specs=[smem()] + [vmem()] * 5,
        out_specs=(vmem(), vmem()),
        compiler_params=limit(24),
        cost_estimate=cost(3),
        name="tail_a",
    )(valid, other, query, hidden, weight, own_attended)


def tail_b_kernel(attended, hidden_ref, weight, residual):
    half, features = attended.shape
    project_columns(attended, hidden_ref.at[half:, :], weight, residual, SPLIT, features)


def tail_b(attended, hidden, weight):
    half, features = attended.shape
    return pl.pallas_call(
        tail_b_kernel,
        out_shape=jax.ShapeDtypeStruct((half, features - SPLIT), jnp.bfloat16),
        in_specs=[vmem()] * 3,
        out_specs=vmem(),
        compiler_params=limit(24),
        cost_estimate=cost(1),
        name="tail_b",
    )(attended, hidden, weight)


def head_kernel(
    valid_ref,
    own_ref,
    other_ref,
    query_ref,
    hidden_ref,
    weight,
    gain_ref,
    left_ref,
    right_ref,
    taps_ref,
    out_ref,
    residual,
    partial_ref,
    attended,
):
    count, features = residual.shape
    step = count // 2
    attend_rows(valid_ref, own_ref, other_ref, query_ref.at[:count, :], 0, attended)
    project_columns(attended, hidden_ref.at[:count, :], weight, residual, 0, features)
    head, tail = (residual,), (left_ref, right_ref)
    head_inverse, tail_inverse = inverse_of(head), inverse_of(tail)
    for s in range(0, features, LANES):
        w = min(LANES, features - s)
        taps = [taps_ref[j : j + 1, s : s + w] for j in range(3)]
        early = normed_at(head, head_inverse, gain_ref, s, w)
        late = normed_at(tail, tail_inverse, gain_ref, s, w)
        frames = [early[:step], early[step:], late[:step], late[step:]]
        partial_ref[:step, s : s + w] = taps[0] * frames[0]
        partial_ref[step:, s : s + w] = taps[0] * frames[1] + taps[1] * frames[0]
        here = at_columns(tail, s, w)
        for t in range(2):
            total = taps[0] * frames[t + 2] + taps[1] * frames[t + 1] + taps[2] * frames[t]
            temporal = total.astype(jnp.bfloat16).astype(jnp.float32)
            at = slice(t * step, (t + 1) * step)
            out_ref[at, s : s + w] = (here[at] + temporal).astype(jnp.bfloat16)


def head_of(valid, own, other, query, hidden, weight, gain, left, right, taps):
    tokens, features = query.shape
    half = (tokens // 2, features)
    return pl.pallas_call(
        head_kernel,
        grid=(1,),
        out_shape=(
            jax.ShapeDtypeStruct(query.shape, jnp.bfloat16),
            jax.ShapeDtypeStruct(half, jnp.bfloat16),
            jax.ShapeDtypeStruct(half, jnp.float32),
        ),
        in_specs=[smem()] + [vmem()] * 9,
        out_specs=(pl.BlockSpec(half, lambda i: (1, 0)), vmem(), vmem()),
        scratch_shapes=[pltpu.VMEM(half, jnp.bfloat16)],
        compiler_params=limit(24),
        cost_estimate=cost(3),
        name="head_of",
    )(valid, own, other, query, hidden, weight, gain, left, right, taps)


def finish_kernel(
    unused_ref, residual_ref, partial_ref, left_ref, right_ref, gain_ref, taps_ref, out_ref
):
    count, features = residual_ref.shape
    step = count // 2
    halo = (left_ref, right_ref)
    inverse = inverse_of(halo)
    for s in range(0, features, LANES):
        w = min(LANES, features - s)
        taps = [taps_ref[j : j + 1, s : s + w] for j in range(3)]
        before = normed_at(halo, inverse, gain_ref, s, w)
        oldest, older = before[:step], before[step:]
        totals = [
            partial_ref[:step, s : s + w] + taps[1] * older + taps[2] * oldest,
            partial_ref[step:, s : s + w] + taps[2] * older,
        ]
        for t, total in enumerate(totals):
            temporal = total.astype(jnp.bfloat16).astype(jnp.float32)
            at = slice(t * step, (t + 1) * step)
            here = residual_ref[at, s : s + w].astype(jnp.float32)
            out_ref[at, s : s + w] = (here + temporal).astype(jnp.bfloat16)


def finish(out, residual, partial, left, right, gain, taps):
    return pl.pallas_call(
        finish_kernel,
        grid=(1,),
        out_shape=jax.ShapeDtypeStruct(out.shape, out.dtype),
        in_specs=[pl.BlockSpec(memory_space=pl.ANY)] + [vmem()] * 6,
        out_specs=pl.BlockSpec(residual.shape, lambda i: (0, 0)),
        input_output_aliases={0: 0},
        compiler_params=limit(8),
        cost_estimate=cost(1),
        name="finish",
    )(out, residual, partial, left, right, gain, taps)


def body(query_in, key_in, value_in, hidden_in, out_weight, norm_gain, temporal_taps, block_valid):
    frames, rows_dev, width_cols, features = query_in.shape
    tokens = frames * rows_dev * width_cols
    query = query_in.reshape(tokens, features)
    hidden = hidden_in.reshape(tokens, features)
    swap = [(0, 1), (1, 0)]
    value = value_in.reshape(tokens, features)
    turned = turn(live_of(block_valid, tokens), key_in.reshape(tokens, features))
    send = local_states(turned, value, False)
    fetched = lax.ppermute(send, "core", swap)
    keep = local_states(turned, value, True)
    mine = (keep + fetched.astype(jnp.float32)).astype(jnp.bfloat16)
    piece = ROWS // (Z * Y)
    got = lax.all_to_all(mine, ("z", "y"), 0, 0, tiled=True).reshape(Z * Y, piece, LANES)
    prefix, whole = prefixes(got)
    wholes = lax.all_to_all(whole, "x", 0, 0, tiled=True)
    own = lax.all_to_all(totals(prefix, wholes), ("z", "y"), 0, 0, tiled=True)
    own = own.reshape(ROWS, LANES)
    other = lax.ppermute(own, "core", swap)
    own_attended = tail_own(block_valid, own, query)
    gain = norm_gain.reshape(1, features)
    shared = (block_valid, own, other, query, hidden, out_weight)
    chain = [(i, i + 1) for i in range(X * Z - 1)]
    attended, left = tail_a(block_valid, other, query, hidden, out_weight, own_attended)
    halo_left = lax.ppermute(left, ("x", "z"), chain)
    right = tail_b(attended, hidden, out_weight)
    halo_right = lax.ppermute(right, ("x", "z"), chain)
    out, residual, partial = head_of(*shared, gain, left, right, temporal_taps)
    mixed = finish(out, residual, partial, halo_left, halo_right, gain, temporal_taps)
    return mixed.reshape(query_in.shape)


def solution(mesh):
    fine = Mesh(mesh.devices.reshape(X, Z, Y, C), ("x", "z", "y", "core"))
    token = P(("x", "z"), ("y", "core"), None, None)
    placed = (token, token, token, token, P(), P(), P(), P(("x", "z")))

    return jax.shard_map(body, mesh=fine, in_specs=placed, out_specs=token, check_vma=False)
```

```python
import functools

import jax
import jax.numpy as jnp
from jax import lax
from jax.experimental import pallas as pl
from jax.experimental.pallas import tpu as pltpu
from jax.sharding import Mesh, PartitionSpec as P


HEADS = 20
DH = 112
LANES = 128
PIECE = 14
GROUP = HEADS // 2
ROWS = 1024
EPS_DEN = 1e-06
EPS_NORM = 1e-06
X, Z, Y, C = 4, 8, 4, 2
CHUNK = 512
SPLIT = 1408


def smem():
    return pl.BlockSpec(memory_space=pltpu.SMEM)


def vmem():
    return pl.BlockSpec(memory_space=pltpu.VMEM)


def limit(mib):
    return pltpu.CompilerParams(vmem_limit_bytes=mib << 20)


def cost(micros):
    return pl.CostEstimate(flops=micros * 1_000_000_000, bytes_accessed=1 << 20, transcendentals=0)


def lane_of(shape):
    return lax.broadcasted_iota(jnp.int32, shape, 1)


def place_of(h):
    return (h * DH) // LANES, (h * DH) % LANES


def free_of(h):
    return ((h + 1) * DH) % LANES


def group_states(group, turned, value_ref, out_ref):
    tokens, features = value_ref.shape
    lane = lane_of((tokens, LANES))
    one = jnp.ones((tokens, LANES), jnp.bfloat16)
    lanes = lane_of((DH, LANES))

    def values_at(start):
        width = min(LANES, features - start)
        values = value_ref[:, start : start + width]
        if width < LANES:
            values = jnp.concatenate(
                [values, jnp.zeros((tokens, LANES - width), jnp.bfloat16)], axis=1
            )
        return values

    def head(h):
        tile, off = place_of(h)
        keys = turned[h * DH : (h + 1) * DH, :]
        low = values_at(tile * LANES)
        if off == 0:
            low = jnp.where(lane == DH, one, low)
            return jnp.dot(keys, low, preferred_element_type=jnp.float32)
        high = jnp.where(lane == free_of(h), one, values_at((tile + 1) * LANES))
        wide = jnp.dot(
            keys, jnp.concatenate([low, high], axis=1), preferred_element_type=jnp.float32
        )
        return jnp.where(lanes >= off, wide[:, :LANES], wide[:, LANES:])

    end = group * GROUP + GROUP - 1
    last = head(end)
    for p in range(GROUP - 1):
        h = group * GROUP + p
        free = free_of(h)
        state = head(h)
        if p < 8:
            shift = (free + 2 - place_of(end)[1] - PIECE * p) % LANES
            mask = (lanes >= free + 2) & (lanes < free + 16)
        else:
            shift = (free + 1 - free_of(end)) % LANES
            mask = lanes == free + 1
        moved = pltpu.roll(last, shift, axis=1) if shift else last
        state = jnp.where(mask, moved, state)
        out_ref[p * DH : (p + 1) * DH, :] = state.astype(out_ref.dtype)
    rest = ROWS - (GROUP - 1) * DH
    out_ref[(GROUP - 1) * DH :, :] = jnp.zeros((rest, LANES), out_ref.dtype)


def live_kernel(valid_ref, out_ref):
    tokens = out_ref.shape[0]
    row = lax.broadcasted_iota(jnp.int32, out_ref.shape, 0)
    live = row < valid_ref[0] * (tokens // 4)
    out_ref[...] = jnp.where(live, 1.0, 0.0).astype(jnp.bfloat16)


def live_of(valid, tokens):
    return pl.pallas_call(
        live_kernel,
        out_shape=jax.ShapeDtypeStruct((tokens, LANES), jnp.bfloat16),
        in_specs=[smem()],
        out_specs=vmem(),
        compiler_params=limit(2),
        cost_estimate=cost(8),
        name="live_of",
    )(valid)


def turn_kernel(live_ref, key_ref, out_ref):
    _, features = key_ref.shape
    live = live_ref[...]
    for start in range(0, features, LANES):
        width = min(LANES, features - start)
        keys = jnp.maximum(key_ref[:, start : start + width], 0) * live[:, :width]
        out_ref[start : start + width, :] = keys.T


def turn(live, key):
    tokens, features = key.shape
    return pl.pallas_call(
        turn_kernel,
        out_shape=jax.ShapeDtypeStruct((features, tokens), jnp.bfloat16),
        in_specs=[vmem(), vmem()],
        out_specs=vmem(),
        compiler_params=limit(8),
        name="turn",
    )(live, key)


def state_kernel(mine, turned, value_ref, out_ref):
    core = lax.axis_index("core")
    for group in range(2):

        @pl.when(core == (group if mine else 1 - group))
        def _():
            group_states(group, turned, value_ref, out_ref)


def local_states(turned, value, mine):
    return pl.pallas_call(
        functools.partial(state_kernel, mine),
        out_shape=jax.ShapeDtypeStruct((ROWS, LANES), jnp.float32 if mine else jnp.bfloat16),
        in_specs=[vmem(), vmem()],
        out_specs=vmem(),
        compiler_params=limit(8),
        cost_estimate=cost(1),
        name="kept_states" if mine else "sent_states",
    )(turned, value)


def prefix_kernel(got_ref, prefix_ref, whole_ref):
    total = jnp.zeros(prefix_ref.shape[1:], jnp.float32)
    for z in range(Z):
        for y in range(Y):
            total = total + got_ref[z * Y + y].astype(jnp.float32)
        prefix_ref[z] = total
    for x in range(X):
        whole_ref[x] = total


def prefixes(got):
    piece = got.shape[1:]
    return pl.pallas_call(
        prefix_kernel,
        out_shape=(
            jax.ShapeDtypeStruct((Z,) + piece, jnp.float32),
            jax.ShapeDtypeStruct((X,) + piece, jnp.float32),
        ),
        in_specs=[vmem()],
        out_specs=(vmem(), vmem()),
        compiler_params=limit(4),
        cost_estimate=cost(8),
        name="prefixes",
    )(got)


def totals_kernel(prefix_ref, whole_ref, out_ref):
    place = lax.axis_index("x")
    before = jnp.zeros(prefix_ref.shape[1:], jnp.float32)
    for x in range(X):
        before = before + jnp.where(x < place, whole_ref[x], 0.0)
    for z in range(Z):
        total = (prefix_ref[z] + before).astype(jnp.bfloat16)
        for y in range(Y):
            out_ref[z * Y + y] = total


def totals(prefix, whole):
    piece = prefix.shape[1:]
    return pl.pallas_call(
        totals_kernel,
        out_shape=jax.ShapeDtypeStruct((Z * Y,) + piece, jnp.bfloat16),
        in_specs=[vmem(), vmem()],
        out_specs=vmem(),
        compiler_params=limit(4),
        cost_estimate=cost(8),
        name="totals",
    )(prefix, whole)


def unpack(group, stored):
    lanes = lane_of((DH, LANES))
    packed = [stored(group, p) for p in range(GROUP - 1)]
    end = group * GROUP + GROUP - 1
    off = place_of(end)[1]
    last = jnp.zeros((DH, LANES), jnp.float32)
    for p in range(GROUP - 1):
        free = free_of(group * GROUP + p)
        if p < 8:
            shift = (off + PIECE * p - free - 2) % LANES
            start = (off + PIECE * p) % LANES
            mask = (lanes >= start) & (lanes < start + PIECE)
            if start + PIECE > LANES:
                mask = mask | (lanes < start + PIECE - LANES)
        else:
            shift = (free_of(end) - free - 1) % LANES
            mask = lanes == free_of(end)
        wide = packed[p].astype(jnp.float32)
        moved = pltpu.roll(wide, shift, axis=1) if shift else wide
        last = jnp.where(mask, moved, last)
    return packed + [last.astype(jnp.bfloat16)]


def window(h, packed):
    lanes = lane_of((DH, LANES))
    zero = jnp.zeros((DH, LANES), jnp.bfloat16)
    off = place_of(h)[1]
    if off == 0:
        return jnp.where(lanes <= DH, packed, zero)
    low = jnp.where(lanes >= off, packed, zero)
    high = jnp.where(lanes <= off - 16, packed, zero)
    return jnp.concatenate([low, high], axis=1)


def attend_group(group, stored, query_ref, live, attended, carry):
    count, features = query_ref.shape
    lane = lane_of((count, LANES))
    unpacked = unpack(group, stored)
    for p in range(GROUP):
        h = group * GROUP + p
        tile, off = place_of(h)
        start = tile * LANES
        stop = min(start + (LANES if off == 0 else 2 * LANES), features)
        wide = window(h, unpacked[p])
        parts = [wide]
        if off:
            parts.insert(0, jnp.zeros((off, wide.shape[1]), jnp.bfloat16))
        rest = stop - start - off - DH
        if rest:
            parts.append(jnp.zeros((rest, wide.shape[1]), jnp.bfloat16))
        matrix = jnp.concatenate(parts, axis=0) if len(parts) > 1 else wide
        query = jnp.maximum(query_ref[:, start:stop], 0)
        got = jnp.dot(query, matrix, preferred_element_type=jnp.float32)
        below = got[:, off + DH : off + DH + 1] + EPS_DEN
        scale = jnp.broadcast_to(live / below, (count, LANES))
        low = got[:, :LANES] * scale
        if off == 0:
            carry = low
            continue
        full = jnp.where(lane >= off, low, carry)
        attended[:, start : start + LANES] = full.astype(jnp.bfloat16)
        carry = got[:, LANES:] * scale
    return carry


def live_rows(valid_ref, count, first):
    step = count // 2
    row = lax.broadcasted_iota(jnp.int32, (count, 1), 0)
    return (row + first * step < valid_ref[0] * step).astype(jnp.float32)


def store_end(attended, carry):
    left = attended.shape[1] % LANES
    if left:
        attended[:, attended.shape[1] - left :] = carry[:, :left].astype(jnp.bfloat16)


def attend_rows(valid_ref, own_ref, other_ref, query_ref, first, attended):
    own = lax.axis_index("core")

    def stored(group, p):
        at = slice(p * DH, (p + 1) * DH)
        return jnp.where(own == group, own_ref[at, :], other_ref[at, :])

    live = live_rows(valid_ref, query_ref.shape[0], first)
    carry = None
    for group in range(2):
        carry = attend_group(group, stored, query_ref, live, attended, carry)
    store_end(attended, carry)


def attend_half(group, valid_ref, state_ref, query_ref, attended):
    count = query_ref.shape[0]

    def stored(group, p):
        return state_ref[p * DH : (p + 1) * DH, :]

    live = live_rows(valid_ref, count, 2)
    carry = jnp.zeros((count, LANES), jnp.float32)
    carry = attend_group(group, stored, query_ref, live, attended, carry)
    if group:
        store_end(attended, carry)
    else:
        tile = place_of(GROUP)[0] * LANES
        attended[:, tile : tile + LANES] = carry.astype(jnp.bfloat16)


def tail_own_kernel(valid_ref, own_ref, query_ref, attended):
    half = query_ref.shape[0] // 2
    core = lax.axis_index("core")
    for group in range(2):

        @pl.when(core == group)
        def _():
            attend_half(group, valid_ref, own_ref, query_ref.at[half:, :], attended)


def tail_own(valid, own, query):
    tokens, features = query.shape
    return pl.pallas_call(
        tail_own_kernel,
        out_shape=jax.ShapeDtypeStruct((tokens // 2, features), jnp.bfloat16),
        in_specs=[smem(), vmem(), vmem()],
        out_specs=vmem(),
        compiler_params=limit(8),
        cost_estimate=cost(1),
        name="tail_own",
    )(valid, own, query)


def project_columns(attended, hidden_ref, weight, residual, start, stop):
    for s in range(start, stop, CHUNK):
        at = slice(s, min(s + CHUNK, stop))
        projected = jnp.dot(attended[...], weight[:, at], preferred_element_type=jnp.float32)
        rounded = (hidden_ref[:, at].astype(jnp.float32) + projected).astype(jnp.bfloat16)
        residual[:, at.start - start : at.stop - start] = rounded


def inverse_of(parts):
    count = parts[0].shape[0]
    features = sum(part.shape[1] for part in parts)
    squares = jnp.zeros((count, LANES), jnp.float32)
    for part in parts:
        width = part.shape[1]
        for s in range(0, width, LANES):
            w = min(LANES, width - s)
            wide = part[:, s : s + w].astype(jnp.float32)
            wide = wide * wide
            if w < LANES:
                wide = jnp.concatenate([wide, jnp.zeros((count, LANES - w), jnp.float32)], axis=1)
            squares = squares + wide
    mean = jnp.sum(squares, axis=1, keepdims=True) / features
    return jnp.broadcast_to(lax.rsqrt(mean + EPS_NORM), (count, LANES))


def normed_at(parts, inverse, gain_ref, s, w):
    here = at_columns(parts, s, w)
    normed = (here * inverse[:, :w] * gain_ref[:, s : s + w]).astype(jnp.bfloat16)
    return normed.astype(jnp.float32)


def at_columns(parts, s, w):
    for part in parts:
        if s < part.shape[1]:
            return part[:, s : s + w].astype(jnp.float32)
        s -= part.shape[1]


def tail_a_kernel(
    valid_ref, other_ref, query_ref, hidden_ref, weight, own_attended, attended, residual
):
    count, features = attended.shape
    core = lax.axis_index("core")
    tile, off = place_of(GROUP)
    shared = slice(tile * LANES, (tile + 1) * LANES)
    lane = lane_of((count, LANES))
    for group in range(2):

        @pl.when(core == 1 - group)
        def _():
            attend_half(group, valid_ref, other_ref, query_ref.at[count:, :], attended)
            done = slice(shared.stop, features) if group == 0 else slice(0, shared.start)
            attended[:, done] = own_attended[:, done]
            first = (attended if group == 0 else own_attended)[:, shared]
            second = (own_attended if group == 0 else attended)[:, shared]
            attended[:, shared] = jnp.where(lane < off, first, second)

    project_columns(attended, hidden_ref.at[count:, :], weight, residual, 0, SPLIT)


def tail_a(valid, other, query, hidden, weight, own_attended):
    tokens, features = query.shape
    return pl.pallas_call(
        tail_a_kernel,
        out_shape=(
            jax.ShapeDtypeStruct((tokens // 2, features), jnp.bfloat16),
            jax.ShapeDtypeStruct((tokens // 2, SPLIT), jnp.bfloat16),
        ),
        in_specs=[smem()] + [vmem()] * 5,
        out_specs=(vmem(), vmem()),
        compiler_params=limit(24),
        cost_estimate=cost(3),
        name="tail_a",
    )(valid, other, query, hidden, weight, own_attended)


def tail_b_kernel(attended, hidden_ref, weight, left_ref, right_ref, residual):
    half, features = attended.shape
    project_columns(attended, hidden_ref.at[half:, :], weight, right_ref, SPLIT, features)
    residual[:, :SPLIT] = left_ref[...]
    residual[:, SPLIT:] = right_ref[...]


def tail_b(attended, hidden, weight, left):
    half, features = attended.shape
    return pl.pallas_call(
        tail_b_kernel,
        out_shape=(
            jax.ShapeDtypeStruct((half, features - SPLIT), jnp.bfloat16),
            jax.ShapeDtypeStruct((half, features), jnp.bfloat16),
        ),
        in_specs=[vmem()] * 4,
        out_specs=(vmem(), vmem()),
        compiler_params=limit(24),
        cost_estimate=cost(1),
        name="tail_b",
    )(attended, hidden, weight, left)


def head_kernel(
    valid_ref,
    own_ref,
    other_ref,
    query_ref,
    hidden_ref,
    weight,
    gain_ref,
    tail_ref,
    taps_ref,
    out_ref,
    residual,
    partial_ref,
    attended,
):
    count, features = residual.shape
    step = count // 2
    attend_rows(valid_ref, own_ref, other_ref, query_ref.at[:count, :], 0, attended)
    project_columns(attended, hidden_ref.at[:count, :], weight, residual, 0, features)
    head, tail = (residual,), (tail_ref,)
    head_inverse, tail_inverse = inverse_of(head), inverse_of(tail)
    for s in range(0, features, LANES):
        w = min(LANES, features - s)
        taps = [taps_ref[j : j + 1, s : s + w] for j in range(3)]
        early = normed_at(head, head_inverse, gain_ref, s, w)
        late = normed_at(tail, tail_inverse, gain_ref, s, w)
        frames = [early[:step], early[step:], late[:step], late[step:]]
        partial_ref[:step, s : s + w] = taps[0] * frames[0]
        partial_ref[step:, s : s + w] = taps[0] * frames[1] + taps[1] * frames[0]
        here = at_columns(tail, s, w)
        for t in range(2):
            total = taps[0] * frames[t + 2] + taps[1] * frames[t + 1] + taps[2] * frames[t]
            temporal = total.astype(jnp.bfloat16).astype(jnp.float32)
            at = slice(t * step, (t + 1) * step)
            out_ref[at, s : s + w] = (here[at] + temporal).astype(jnp.bfloat16)


def head_of(valid, own, other, query, hidden, weight, gain, tail, taps):
    tokens, features = query.shape
    half = (tokens // 2, features)
    return pl.pallas_call(
        head_kernel,
        grid=(1,),
        out_shape=(
            jax.ShapeDtypeStruct(query.shape, jnp.bfloat16),
            jax.ShapeDtypeStruct(half, jnp.bfloat16),
            jax.ShapeDtypeStruct(half, jnp.float32),
        ),
        in_specs=[smem()] + [vmem()] * 8,
        out_specs=(pl.BlockSpec(half, lambda i: (1, 0)), vmem(), vmem()),
        scratch_shapes=[pltpu.VMEM(half, jnp.bfloat16)],
        compiler_params=limit(24),
        cost_estimate=cost(3),
        name="head_of",
    )(valid, own, other, query, hidden, weight, gain, tail, taps)


def finish_kernel(
    unused_ref, residual_ref, partial_ref, near_ref, left_ref, right_ref, gain_ref, taps_ref, out_ref, both
):
    count, features = residual_ref.shape
    step = count // 2
    edge = lax.axis_index("z") == 0
    both[:, :SPLIT] = jnp.where(edge, left_ref[...], near_ref[:, :SPLIT])
    both[:, SPLIT:] = jnp.where(edge, right_ref[...], near_ref[:, SPLIT:])
    halo = (both,)
    inverse = inverse_of(halo)
    for s in range(0, features, LANES):
        w = min(LANES, features - s)
        taps = [taps_ref[j : j + 1, s : s + w] for j in range(3)]
        before = normed_at(halo, inverse, gain_ref, s, w)
        oldest, older = before[:step], before[step:]
        totals = [
            partial_ref[:step, s : s + w] + taps[1] * older + taps[2] * oldest,
            partial_ref[step:, s : s + w] + taps[2] * older,
        ]
        for t, total in enumerate(totals):
            temporal = total.astype(jnp.bfloat16).astype(jnp.float32)
            at = slice(t * step, (t + 1) * step)
            here = residual_ref[at, s : s + w].astype(jnp.float32)
            out_ref[at, s : s + w] = (here + temporal).astype(jnp.bfloat16)


def finish(out, residual, partial, near, left, right, gain, taps):
    return pl.pallas_call(
        finish_kernel,
        grid=(1,),
        out_shape=jax.ShapeDtypeStruct(out.shape, out.dtype),
        in_specs=[pl.BlockSpec(memory_space=pl.ANY)] + [vmem()] * 7,
        out_specs=pl.BlockSpec(residual.shape, lambda i: (0, 0)),
        scratch_shapes=[pltpu.VMEM(residual.shape, jnp.bfloat16)],
        input_output_aliases={0: 0},
        compiler_params=limit(8),
        cost_estimate=cost(1),
        name="finish",
    )(out, residual, partial, near, left, right, gain, taps)


def body(query_in, key_in, value_in, hidden_in, out_weight, norm_gain, temporal_taps, block_valid):
    frames, rows_dev, width_cols, features = query_in.shape
    tokens = frames * rows_dev * width_cols
    query = query_in.reshape(tokens, features)
    hidden = hidden_in.reshape(tokens, features)
    swap = [(0, 1), (1, 0)]
    value = value_in.reshape(tokens, features)
    turned = turn(live_of(block_valid, tokens), key_in.reshape(tokens, features))
    send = local_states(turned, value, False)
    fetched = lax.ppermute(send, "core", swap)
    keep = local_states(turned, value, True)
    mine = (keep + fetched.astype(jnp.float32)).astype(jnp.bfloat16)
    piece = ROWS // (Z * Y)
    got = lax.all_to_all(mine, ("z", "y"), 0, 0, tiled=True).reshape(Z * Y, piece, LANES)
    prefix, whole = prefixes(got)
    wholes = lax.all_to_all(whole, "x", 0, 0, tiled=True)
    own = lax.all_to_all(totals(prefix, wholes), ("z", "y"), 0, 0, tiled=True)
    own = own.reshape(ROWS, LANES)
    other = lax.ppermute(own, "core", swap)
    own_attended = tail_own(block_valid, own, query)
    gain = norm_gain.reshape(1, features)
    shared = (block_valid, own, other, query, hidden, out_weight)
    chain = [(i, i + 1) for i in range(X * Z - 1)]
    within = [pair for pair in chain if pair[1] % Z]
    across = [pair for pair in chain if pair[1] % Z == 0]
    attended, left = tail_a(block_valid, other, query, hidden, out_weight, own_attended)
    edge_left = lax.ppermute(left, ("x", "z"), across)
    right, tail = tail_b(attended, hidden, out_weight, left)
    edge_right = lax.ppermute(right, ("x", "z"), across)
    near = lax.ppermute(tail, ("x", "z"), within)
    out, residual, partial = head_of(*shared, gain, tail, temporal_taps)
    mixed = finish(out, residual, partial, near, edge_left, edge_right, gain, temporal_taps)
    return mixed.reshape(query_in.shape)


def solution(mesh):
    fine = Mesh(mesh.devices.reshape(X, Z, Y, C), ("x", "z", "y", "core"))
    token = P(("x", "z"), ("y", "core"), None, None)
    placed = (token, token, token, token, P(), P(), P(), P(("x", "z")))

    return jax.shard_map(body, mesh=fine, in_specs=placed, out_specs=token, check_vma=False)
```

```python
import functools

import jax
import jax.numpy as jnp
from jax import lax
from jax.experimental import pallas as pl
from jax.experimental.pallas import tpu as pltpu
from jax.sharding import Mesh, PartitionSpec as P


HEADS = 20
DH = 112
LANES = 128
PIECE = 14
GROUP = HEADS // 2
ROWS = 1024
EPS_DEN = 1e-06
EPS_NORM = 1e-06
X, Z, Y, C = 4, 8, 4, 2
CHUNK = 512
SPLIT = 1408


def smem():
    return pl.BlockSpec(memory_space=pltpu.SMEM)


def vmem():
    return pl.BlockSpec(memory_space=pltpu.VMEM)


def limit(mib):
    return pltpu.CompilerParams(vmem_limit_bytes=mib << 20)


def cost(micros):
    return pl.CostEstimate(flops=micros * 1_000_000_000, bytes_accessed=1 << 20, transcendentals=0)


def lane_of(shape):
    return lax.broadcasted_iota(jnp.int32, shape, 1)


def place_of(h):
    return (h * DH) // LANES, (h * DH) % LANES


def free_of(h):
    return ((h + 1) * DH) % LANES


def group_states(group, turned, value_ref, out_ref):
    tokens, features = value_ref.shape
    lane = lane_of((tokens, LANES))
    one = jnp.ones((tokens, LANES), jnp.bfloat16)
    lanes = lane_of((DH, LANES))

    def values_at(start):
        width = min(LANES, features - start)
        values = value_ref[:, start : start + width]
        if width < LANES:
            values = jnp.concatenate(
                [values, jnp.zeros((tokens, LANES - width), jnp.bfloat16)], axis=1
            )
        return values

    def head(h):
        tile, off = place_of(h)
        keys = turned[h * DH : (h + 1) * DH, :]
        low = values_at(tile * LANES)
        if off == 0:
            low = jnp.where(lane == DH, one, low)
            return jnp.dot(keys, low, preferred_element_type=jnp.float32)
        high = jnp.where(lane == free_of(h), one, values_at((tile + 1) * LANES))
        wide = jnp.dot(
            keys, jnp.concatenate([low, high], axis=1), preferred_element_type=jnp.float32
        )
        return jnp.where(lanes >= off, wide[:, :LANES], wide[:, LANES:])

    end = group * GROUP + GROUP - 1
    last = head(end)
    for p in range(GROUP - 1):
        h = group * GROUP + p
        free = free_of(h)
        state = head(h)
        if p < 8:
            shift = (free + 2 - place_of(end)[1] - PIECE * p) % LANES
            mask = (lanes >= free + 2) & (lanes < free + 16)
        else:
            shift = (free + 1 - free_of(end)) % LANES
            mask = lanes == free + 1
        moved = pltpu.roll(last, shift, axis=1) if shift else last
        state = jnp.where(mask, moved, state)
        out_ref[p * DH : (p + 1) * DH, :] = state.astype(out_ref.dtype)
    rest = ROWS - (GROUP - 1) * DH
    out_ref[(GROUP - 1) * DH :, :] = jnp.zeros((rest, LANES), out_ref.dtype)


def live_kernel(valid_ref, out_ref):
    tokens = out_ref.shape[0]
    row = lax.broadcasted_iota(jnp.int32, out_ref.shape, 0)
    live = row < valid_ref[0] * (tokens // 4)
    out_ref[...] = jnp.where(live, 1.0, 0.0).astype(jnp.bfloat16)


def live_of(valid, tokens):
    return pl.pallas_call(
        live_kernel,
        out_shape=jax.ShapeDtypeStruct((tokens, LANES), jnp.bfloat16),
        in_specs=[smem()],
        out_specs=vmem(),
        compiler_params=limit(2),
        cost_estimate=cost(8),
        name="live_of",
    )(valid)


def turn_kernel(live_ref, key_ref, out_ref):
    _, features = key_ref.shape
    live = live_ref[...]
    for start in range(0, features, LANES):
        width = min(LANES, features - start)
        keys = jnp.maximum(key_ref[:, start : start + width], 0) * live[:, :width]
        out_ref[start : start + width, :] = keys.T


def turn(live, key):
    tokens, features = key.shape
    return pl.pallas_call(
        turn_kernel,
        out_shape=jax.ShapeDtypeStruct((features, tokens), jnp.bfloat16),
        in_specs=[vmem(), vmem()],
        out_specs=vmem(),
        compiler_params=limit(8),
        name="turn",
    )(live, key)


def state_kernel(mine, turned, value_ref, out_ref):
    core = lax.axis_index("core")
    for group in range(2):

        @pl.when(core == (group if mine else 1 - group))
        def _():
            group_states(group, turned, value_ref, out_ref)


def local_states(turned, value, mine):
    return pl.pallas_call(
        functools.partial(state_kernel, mine),
        out_shape=jax.ShapeDtypeStruct((ROWS, LANES), jnp.float32 if mine else jnp.bfloat16),
        in_specs=[vmem(), vmem()],
        out_specs=vmem(),
        compiler_params=limit(8),
        cost_estimate=cost(1),
        name="kept_states" if mine else "sent_states",
    )(turned, value)


def prefix_kernel(got_ref, prefix_ref, whole_ref):
    total = jnp.zeros(prefix_ref.shape[1:], jnp.float32)
    for z in range(Z):
        for y in range(Y):
            total = total + got_ref[z * Y + y].astype(jnp.float32)
        prefix_ref[z] = total
    for x in range(X):
        whole_ref[x] = total


def prefixes(got):
    piece = got.shape[1:]
    return pl.pallas_call(
        prefix_kernel,
        out_shape=(
            jax.ShapeDtypeStruct((Z,) + piece, jnp.float32),
            jax.ShapeDtypeStruct((X,) + piece, jnp.float32),
        ),
        in_specs=[vmem()],
        out_specs=(vmem(), vmem()),
        compiler_params=limit(4),
        cost_estimate=cost(8),
        name="prefixes",
    )(got)


def totals_kernel(prefix_ref, whole_ref, out_ref):
    place = lax.axis_index("x")
    before = jnp.zeros(prefix_ref.shape[1:], jnp.float32)
    for x in range(X):
        before = before + jnp.where(x < place, whole_ref[x], 0.0)
    for z in range(Z):
        total = (prefix_ref[z] + before).astype(jnp.bfloat16)
        for y in range(Y):
            out_ref[z * Y + y] = total


def totals(prefix, whole):
    piece = prefix.shape[1:]
    return pl.pallas_call(
        totals_kernel,
        out_shape=jax.ShapeDtypeStruct((Z * Y,) + piece, jnp.bfloat16),
        in_specs=[vmem(), vmem()],
        out_specs=vmem(),
        compiler_params=limit(4),
        cost_estimate=cost(8),
        name="totals",
    )(prefix, whole)


def unpack(group, stored):
    lanes = lane_of((DH, LANES))
    packed = [stored(group, p) for p in range(GROUP - 1)]
    end = group * GROUP + GROUP - 1
    off = place_of(end)[1]
    last = jnp.zeros((DH, LANES), jnp.float32)
    for p in range(GROUP - 1):
        free = free_of(group * GROUP + p)
        if p < 8:
            shift = (off + PIECE * p - free - 2) % LANES
            start = (off + PIECE * p) % LANES
            mask = (lanes >= start) & (lanes < start + PIECE)
            if start + PIECE > LANES:
                mask = mask | (lanes < start + PIECE - LANES)
        else:
            shift = (free_of(end) - free - 1) % LANES
            mask = lanes == free_of(end)
        wide = packed[p].astype(jnp.float32)
        moved = pltpu.roll(wide, shift, axis=1) if shift else wide
        last = jnp.where(mask, moved, last)
    return packed + [last.astype(jnp.bfloat16)]


def window(h, packed):
    lanes = lane_of((DH, LANES))
    zero = jnp.zeros((DH, LANES), jnp.bfloat16)
    off = place_of(h)[1]
    if off == 0:
        return jnp.where(lanes <= DH, packed, zero)
    low = jnp.where(lanes >= off, packed, zero)
    high = jnp.where(lanes <= off - 16, packed, zero)
    return jnp.concatenate([low, high], axis=1)


def attend_group(group, stored, query_ref, live, attended, carry):
    count, features = query_ref.shape
    lane = lane_of((count, LANES))
    unpacked = unpack(group, stored)
    for p in range(GROUP):
        h = group * GROUP + p
        tile, off = place_of(h)
        start = tile * LANES
        stop = min(start + (LANES if off == 0 else 2 * LANES), features)
        wide = window(h, unpacked[p])
        parts = [wide]
        if off:
            parts.insert(0, jnp.zeros((off, wide.shape[1]), jnp.bfloat16))
        rest = stop - start - off - DH
        if rest:
            parts.append(jnp.zeros((rest, wide.shape[1]), jnp.bfloat16))
        matrix = jnp.concatenate(parts, axis=0) if len(parts) > 1 else wide
        query = jnp.maximum(query_ref[:, start:stop], 0)
        got = jnp.dot(query, matrix, preferred_element_type=jnp.float32)
        below = got[:, off + DH : off + DH + 1] + EPS_DEN
        scale = jnp.broadcast_to(live / below, (count, LANES))
        low = got[:, :LANES] * scale
        if off == 0:
            carry = low
            continue
        full = jnp.where(lane >= off, low, carry)
        attended[:, start : start + LANES] = full.astype(jnp.bfloat16)
        carry = got[:, LANES:] * scale
    return carry


def live_rows(valid_ref, count, first):
    step = count // 2
    row = lax.broadcasted_iota(jnp.int32, (count, 1), 0)
    return (row + first * step < valid_ref[0] * step).astype(jnp.float32)


def store_end(attended, carry):
    left = attended.shape[1] % LANES
    if left:
        attended[:, attended.shape[1] - left :] = carry[:, :left].astype(jnp.bfloat16)


def attend_rows(valid_ref, own_ref, other_ref, query_ref, first, attended):
    own = lax.axis_index("core")

    def stored(group, p):
        at = slice(p * DH, (p + 1) * DH)
        return jnp.where(own == group, own_ref[at, :], other_ref[at, :])

    live = live_rows(valid_ref, query_ref.shape[0], first)
    carry = None
    for group in range(2):
        carry = attend_group(group, stored, query_ref, live, attended, carry)
    store_end(attended, carry)


def attend_half(group, valid_ref, state_ref, query_ref, attended):
    count = query_ref.shape[0]

    def stored(group, p):
        return state_ref[p * DH : (p + 1) * DH, :]

    live = live_rows(valid_ref, count, 2)
    carry = jnp.zeros((count, LANES), jnp.float32)
    carry = attend_group(group, stored, query_ref, live, attended, carry)
    if group:
        store_end(attended, carry)
    else:
        tile, off = place_of(GROUP)
        kept = jnp.where(lane_of((count, LANES)) < off, carry, 0.0)
        attended[:, tile * LANES : (tile + 1) * LANES] = kept.astype(jnp.bfloat16)


def project_columns(attended, hidden_ref, weight, residual, start, stop):
    for s in range(start, stop, CHUNK):
        at = slice(s, min(s + CHUNK, stop))
        projected = jnp.dot(attended[...], weight[:, at], preferred_element_type=jnp.float32)
        rounded = (hidden_ref[:, at].astype(jnp.float32) + projected).astype(jnp.bfloat16)
        residual[:, at.start - start : at.stop - start] = rounded


def inverse_of(parts):
    count = parts[0].shape[0]
    features = sum(part.shape[1] for part in parts)
    squares = jnp.zeros((count, LANES), jnp.float32)
    for part in parts:
        width = part.shape[1]
        for s in range(0, width, LANES):
            w = min(LANES, width - s)
            wide = part[:, s : s + w].astype(jnp.float32)
            wide = wide * wide
            if w < LANES:
                wide = jnp.concatenate([wide, jnp.zeros((count, LANES - w), jnp.float32)], axis=1)
            squares = squares + wide
    mean = jnp.sum(squares, axis=1, keepdims=True) / features
    return jnp.broadcast_to(lax.rsqrt(mean + EPS_NORM), (count, LANES))


def normed_at(parts, inverse, gain_ref, s, w):
    here = at_columns(parts, s, w)
    normed = (here * inverse[:, :w] * gain_ref[:, s : s + w]).astype(jnp.bfloat16)
    return normed.astype(jnp.float32)


def at_columns(parts, s, w):
    for part in parts:
        if s < part.shape[1]:
            return part[:, s : s + w].astype(jnp.float32)
        s -= part.shape[1]


def rows_of(group, features):
    edge = place_of(GROUP)[0] * LANES
    return slice(edge, features) if group else slice(0, edge + LANES)


def partial_product(group, attended, weight, start, stop):
    rows = rows_of(group, weight.shape[0])
    return jnp.dot(
        attended[:, rows], weight[rows, start:stop], preferred_element_type=jnp.float32
    )


def tail_own_kernel(valid_ref, own_ref, query_ref, weight, summed, attended):
    count, features = summed.shape
    core = lax.axis_index("core")
    for group in range(2):

        @pl.when(core == group)
        def _():
            attend_half(group, valid_ref, own_ref, query_ref.at[count:, :], attended)
            for s in range(0, features, CHUNK):
                e = min(s + CHUNK, features)
                summed[:, s:e] = partial_product(group, attended, weight, s, e)


def tail_own(valid, own, query, weight):
    tokens, features = query.shape
    half = (tokens // 2, features)
    return pl.pallas_call(
        tail_own_kernel,
        out_shape=jax.ShapeDtypeStruct(half, jnp.float32),
        in_specs=[smem(), vmem(), vmem(), vmem()],
        out_specs=vmem(),
        scratch_shapes=[pltpu.VMEM(half, jnp.bfloat16)],
        compiler_params=limit(24),
        cost_estimate=cost(1),
        name="tail_own",
    )(valid, own, query, weight)


def add_columns(group, attended, summed, hidden_ref, weight, residual, start, stop):
    for s in range(start, stop, CHUNK):
        at = slice(s, min(s + CHUNK, stop))
        projected = summed[:, at] + partial_product(group, attended, weight, at.start, at.stop)
        rounded = (hidden_ref[:, at].astype(jnp.float32) + projected).astype(jnp.bfloat16)
        residual[:, at.start - start : at.stop - start] = rounded


def tail_a_kernel(
    valid_ref, other_ref, query_ref, hidden_ref, weight, summed, attended, residual
):
    count = attended.shape[0]
    core = lax.axis_index("core")
    for group in range(2):

        @pl.when(core == 1 - group)
        def _():
            attend_half(group, valid_ref, other_ref, query_ref.at[count:, :], attended)
            add_columns(
                group, attended, summed, hidden_ref.at[count:, :], weight, residual, 0, SPLIT
            )


def tail_a(valid, other, query, hidden, weight, summed):
    tokens, features = query.shape
    return pl.pallas_call(
        tail_a_kernel,
        out_shape=(
            jax.ShapeDtypeStruct((tokens // 2, features), jnp.bfloat16),
            jax.ShapeDtypeStruct((tokens // 2, SPLIT), jnp.bfloat16),
        ),
        in_specs=[smem()] + [vmem()] * 5,
        out_specs=(vmem(), vmem()),
        compiler_params=limit(24),
        cost_estimate=cost(3),
        name="tail_a",
    )(valid, other, query, hidden, weight, summed)


def tail_b_kernel(attended, hidden_ref, weight, summed, residual):
    half, features = attended.shape
    core = lax.axis_index("core")
    for group in range(2):

        @pl.when(core == 1 - group)
        def _():
            add_columns(
                group, attended, summed, hidden_ref.at[half:, :], weight, residual, SPLIT, features
            )


def tail_b(attended, hidden, weight, summed):
    half, features = attended.shape
    return pl.pallas_call(
        tail_b_kernel,
        out_shape=jax.ShapeDtypeStruct((half, features - SPLIT), jnp.bfloat16),
        in_specs=[vmem()] * 4,
        out_specs=vmem(),
        compiler_params=limit(24),
        cost_estimate=cost(1),
        name="tail_b",
    )(attended, hidden, weight, summed)


def head_kernel(
    valid_ref,
    own_ref,
    other_ref,
    query_ref,
    hidden_ref,
    weight,
    gain_ref,
    left_ref,
    right_ref,
    taps_ref,
    out_ref,
    residual,
    partial_ref,
    attended,
):
    count, features = residual.shape
    step = count // 2
    attend_rows(valid_ref, own_ref, other_ref, query_ref.at[:count, :], 0, attended)
    project_columns(attended, hidden_ref.at[:count, :], weight, residual, 0, features)
    head, tail = (residual,), (left_ref, right_ref)
    head_inverse, tail_inverse = inverse_of(head), inverse_of(tail)
    for s in range(0, features, LANES):
        w = min(LANES, features - s)
        taps = [taps_ref[j : j + 1, s : s + w] for j in range(3)]
        early = normed_at(head, head_inverse, gain_ref, s, w)
        late = normed_at(tail, tail_inverse, gain_ref, s, w)
        frames = [early[:step], early[step:], late[:step], late[step:]]
        partial_ref[:step, s : s + w] = taps[0] * frames[0]
        partial_ref[step:, s : s + w] = taps[0] * frames[1] + taps[1] * frames[0]
        here = at_columns(tail, s, w)
        for t in range(2):
            total = taps[0] * frames[t + 2] + taps[1] * frames[t + 1] + taps[2] * frames[t]
            temporal = total.astype(jnp.bfloat16).astype(jnp.float32)
            at = slice(t * step, (t + 1) * step)
            out_ref[at, s : s + w] = (here[at] + temporal).astype(jnp.bfloat16)


def head_of(valid, own, other, query, hidden, weight, gain, left, right, taps):
    tokens, features = query.shape
    half = (tokens // 2, features)
    return pl.pallas_call(
        head_kernel,
        grid=(1,),
        out_shape=(
            jax.ShapeDtypeStruct(query.shape, jnp.bfloat16),
            jax.ShapeDtypeStruct(half, jnp.bfloat16),
            jax.ShapeDtypeStruct(half, jnp.float32),
        ),
        in_specs=[smem()] + [vmem()] * 9,
        out_specs=(pl.BlockSpec(half, lambda i: (1, 0)), vmem(), vmem()),
        scratch_shapes=[pltpu.VMEM(half, jnp.bfloat16)],
        compiler_params=limit(24),
        cost_estimate=cost(3),
        name="head_of",
    )(valid, own, other, query, hidden, weight, gain, left, right, taps)


def finish_kernel(
    unused_ref, residual_ref, partial_ref, left_ref, right_ref, gain_ref, taps_ref, out_ref
):
    count, features = residual_ref.shape
    step = count // 2
    halo = (left_ref, right_ref)
    inverse = inverse_of(halo)
    for s in range(0, features, LANES):
        w = min(LANES, features - s)
        taps = [taps_ref[j : j + 1, s : s + w] for j in range(3)]
        before = normed_at(halo, inverse, gain_ref, s, w)
        oldest, older = before[:step], before[step:]
        totals = [
            partial_ref[:step, s : s + w] + taps[1] * older + taps[2] * oldest,
            partial_ref[step:, s : s + w] + taps[2] * older,
        ]
        for t, total in enumerate(totals):
            temporal = total.astype(jnp.bfloat16).astype(jnp.float32)
            at = slice(t * step, (t + 1) * step)
            here = residual_ref[at, s : s + w].astype(jnp.float32)
            out_ref[at, s : s + w] = (here + temporal).astype(jnp.bfloat16)


def finish(out, residual, partial, left, right, gain, taps):
    return pl.pallas_call(
        finish_kernel,
        grid=(1,),
        out_shape=jax.ShapeDtypeStruct(out.shape, out.dtype),
        in_specs=[pl.BlockSpec(memory_space=pl.ANY)] + [vmem()] * 6,
        out_specs=pl.BlockSpec(residual.shape, lambda i: (0, 0)),
        input_output_aliases={0: 0},
        compiler_params=limit(8),
        cost_estimate=cost(1),
        name="finish",
    )(out, residual, partial, left, right, gain, taps)


def body(query_in, key_in, value_in, hidden_in, out_weight, norm_gain, temporal_taps, block_valid):
    frames, rows_dev, width_cols, features = query_in.shape
    tokens = frames * rows_dev * width_cols
    query = query_in.reshape(tokens, features)
    hidden = hidden_in.reshape(tokens, features)
    swap = [(0, 1), (1, 0)]
    value = value_in.reshape(tokens, features)
    turned = turn(live_of(block_valid, tokens), key_in.reshape(tokens, features))
    send = local_states(turned, value, False)
    fetched = lax.ppermute(send, "core", swap)
    keep = local_states(turned, value, True)
    mine = (keep + fetched.astype(jnp.float32)).astype(jnp.bfloat16)
    piece = ROWS // (Z * Y)
    got = lax.all_to_all(mine, ("z", "y"), 0, 0, tiled=True).reshape(Z * Y, piece, LANES)
    prefix, whole = prefixes(got)
    wholes = lax.all_to_all(whole, "x", 0, 0, tiled=True)
    own = lax.all_to_all(totals(prefix, wholes), ("z", "y"), 0, 0, tiled=True)
    own = own.reshape(ROWS, LANES)
    other = lax.ppermute(own, "core", swap)
    summed = tail_own(block_valid, own, query, out_weight)
    gain = norm_gain.reshape(1, features)
    shared = (block_valid, own, other, query, hidden, out_weight)
    chain = [(i, i + 1) for i in range(X * Z - 1)]
    attended, left = tail_a(block_valid, other, query, hidden, out_weight, summed)
    halo_left = lax.ppermute(left, ("x", "z"), chain)
    right = tail_b(attended, hidden, out_weight, summed)
    halo_right = lax.ppermute(right, ("x", "z"), chain)
    out, residual, partial = head_of(*shared, gain, left, right, temporal_taps)
    mixed = finish(out, residual, partial, halo_left, halo_right, gain, temporal_taps)
    return mixed.reshape(query_in.shape)


def solution(mesh):
    fine = Mesh(mesh.devices.reshape(X, Z, Y, C), ("x", "z", "y", "core"))
    token = P(("x", "z"), ("y", "core"), None, None)
    placed = (token, token, token, token, P(), P(), P(), P(("x", "z")))

    return jax.shard_map(body, mesh=fine, in_specs=placed, out_specs=token, check_vma=False)
```
